128 devices in a mesh: req: 16 (over y, z), mlp: 8 (over x, core).
Axes of the slice: x: 4, y: 4, z: 4, core: 2. Of those that a mesh axis runs over, the one named last changes fastest.
Arguments:
- queries: bfloat16 [2048, 5120], P('req', 'mlp'), may hold values from -6 to 6
- leaf_keys: bfloat16 [2048, 1024], P('req', 'mlp'), may hold values from -6 to 6
- leaf_token_values: bfloat16 [2048, 1024], P('req', 'mlp'), may hold values from -6 to 6
- key_value_pages: bfloat16 [512, 64, 2, 1024], P('req', None, None, 'mlp'), may hold values from -6 to 6
- page_holder: int32 [16, 6, 4], replicated, may hold values from 0 to 15, as said below
- page_slot: int32 [16, 6, 4], replicated, may hold values from 0 to 31
- segment_ids: int32 [2048], P('req'), may hold values from 0 to 7, as said below
- req_parent: int32 [16, 8], P('req'), may hold values from 0 to 3
- mid_parent: int32 [16, 4], P('req'), may hold values from 0 to 1
- node_len: int32 [16, 6], P('req'), may hold values from 1 to 256
- residual: bfloat16 [2048, 5120], P('req'), may hold values from -6 to 6
- out_proj: bfloat16 [5120, 5120], P('mlp'), may hold values from -0.078125 to 0.078125
- norm_gain: float32 [5120], replicated, may hold values from 0.5 to 1.5
- gate_proj: bfloat16 [5120, 13824], P(None, ('req', 'mlp')), may hold values from -0.078125 to 0.078125
- up_proj: bfloat16 [5120, 13824], P(None, ('req', 'mlp')), may hold values from -0.078125 to 0.078125
- down_proj: bfloat16 [13824, 5120], P(('req', 'mlp')), may hold values from -0.0546875 to 0.0546875
- next_gain: float32 [5120], replicated, may hold values from 0.5 to 1.5
- qkv_proj: bfloat16 [5120, 7168], P(None, 'mlp'), may hold values from -0.078125 to 0.078125
- qkv_bias: float32 [7168], P('mlp'), may hold values from -3 to 3
Outputs:
- layer_out: bfloat16 [2048, 5120], P(('req', 'mlp'))
- qkv_out: bfloat16 [2048, 7168], P('req', 'mlp')
The draws below stay inside these ranges and needn't reach their ends.
Inputs may be any that keep to these rules, and one draw needn't show every extreme that they name: `segment_ids`: within each block of 128 tokens of one group the ids never fall, start at 0, and every id 0 to 7 occurs. `page_holder`: in each row (one group's prefix pages) exactly half of the entries name the row's own group; the other entries name other groups, no group more than 1 times in a row, and some group exactly 1 times.
All inputs are finite; a program needn't handle non-finite values.
Results may differ from the reference program's by a relative error of at most 0.02.
Values may be sent and summed in bfloat16 or wider, within the bound.
A program may use at most 192 MiB of HBM per device.

```python
import math
import jax
import jax.numpy as jnp
from jax import lax

D = 5120
QUERY_HEADS = 40
KEY_VALUE_HEADS = 8
HEAD_SIZE = 128
FF = 13824
QUERY_PER_KV = 5
QKV = 7168
TOK_GRP = 128
REQ_DEV = 8
ROOT_DEV = 2
MID_DEV = 4
NODES_DEV = 6
PAGE_TOKENS = 64
NODE_PAGES = 4
NODE_MAX = 256
PAGES_PER_GROUP = 32
QUERY_TOKENS = 2048
N_REQ = 16


def segment_table(key):
    base_offset = jax.random.fold_in(key, 11)

    def one_row(row):
        order = jax.random.permutation(jax.random.fold_in(base_offset, row), TOK_GRP - 1) + 1
        marks = jnp.zeros((TOK_GRP,), jnp.int32).at[order[:REQ_DEV - 1]].set(1)
        return jnp.cumsum(marks).astype(jnp.int32)
    return jax.vmap(one_row)(jnp.arange(N_REQ)).reshape(-1)


def draw_segment_ids(key, part):
    return segment_table(key)


def draw_queries(key, part):
    token_count = N_REQ * TOK_GRP
    base_offset = jnp.clip(jax.random.normal(jax.random.fold_in(key, 32), (token_count, QUERY_HEADS * HEAD_SIZE)), -5.5, 5.5)
    return base_offset.astype(jnp.bfloat16)


def draw_leaf_keys(key, part):
    token_count = N_REQ * TOK_GRP
    base_offset = jnp.clip(jax.random.normal(jax.random.fold_in(key, 42), (token_count, KEY_VALUE_HEADS * HEAD_SIZE)), -5.5, 5.5)
    return base_offset.astype(jnp.bfloat16)


def draw_page_holder(key, part):
    base_offset = jax.random.fold_in(key, 21)
    token_count = NODES_DEV * NODE_PAGES
    half = token_count // 2

    def one_row(row):
        inner = jax.random.fold_in(base_offset, row)
        rank = jax.random.permutation(jax.random.fold_in(inner, 1), token_count)
        offsets = jax.random.permutation(jax.random.fold_in(inner, 2), N_REQ - 1)
        which = jnp.remainder(jnp.maximum(rank - half, 0), N_REQ - 1)
        distant = jnp.remainder(row + 1 + offsets[which], N_REQ)
        return jnp.where(rank < half, row, distant).astype(jnp.int32)
    return jax.vmap(one_row)(jnp.arange(N_REQ)).reshape(N_REQ, NODES_DEV, NODE_PAGES)


def place_ends(result, key, smallest, largest):
    longest = result.shape.index(max(result.shape))
    spots = []
    for shift in (0, 1):
        where = [jax.random.randint(jax.random.fold_in(key, axis), (), 0, length) for axis, length in enumerate(result.shape)]
        where[longest] = (where[longest] + shift) % result.shape[longest]
        spots.append(tuple(where))
    return result.at[spots[0]].set(smallest).at[spots[1]].set(largest)


def levels(rng, shape, split, smallest, largest):
    level = 1.0
    for axis_at, blocks in split:
        steps = jax.random.uniform(jax.random.fold_in(jax.random.fold_in(rng, 6), axis_at), (blocks,), jnp.float32, smallest / len(split), largest / len(split))
        level = level * jnp.repeat(jnp.exp(steps), shape[axis_at] // blocks).reshape((-1,) + (1,) * (len(shape) - 1 - axis_at))
    return level


def bell_draw(own_key, extent, scale, reach, split=(), held_as=jnp.bfloat16):
    drawn = scale * jax.random.normal(own_key, extent, jnp.float32)
    if split:
        drawn = drawn * levels(own_key, extent, split, -0.22, 0.18)
    return jnp.clip(drawn, -reach, reach).astype(held_as)


def setup_inputs(seed: int = 0) -> dict:
    splits = jax.random.split(jax.random.key(seed), 20)
    return {
        "queries": draw_queries(jax.random.fold_in(splits[19], 71), 0),
        "leaf_keys": draw_leaf_keys(jax.random.fold_in(splits[19], 71), 0),
        "leaf_token_values": bell_draw(splits[2], (QUERY_TOKENS, KEY_VALUE_HEADS * HEAD_SIZE), 1.0, 6.0, ((0, 16), (1, 8))),
        "key_value_pages": bell_draw(splits[3], (N_REQ * PAGES_PER_GROUP, PAGE_TOKENS, 2, KEY_VALUE_HEADS * HEAD_SIZE), 1.0, 6.0, ((0, 16), (3, 8))),
        "page_holder": draw_page_holder(jax.random.fold_in(splits[19], 71), 0),
        "page_slot": place_ends(jax.random.randint(splits[5], (N_REQ, NODES_DEV, NODE_PAGES), 0, PAGES_PER_GROUP), jax.random.fold_in(splits[5], 1), 0, PAGES_PER_GROUP - 1).astype(jnp.int32),
        "segment_ids": draw_segment_ids(jax.random.fold_in(splits[19], 71), 0),
        "req_parent": place_ends(jax.random.randint(splits[7], (N_REQ, REQ_DEV), 0, MID_DEV), jax.random.fold_in(splits[7], 1), 0, MID_DEV - 1).astype(jnp.int32),
        "mid_parent": place_ends(jax.random.randint(splits[8], (N_REQ, MID_DEV), 0, ROOT_DEV), jax.random.fold_in(splits[8], 1), 0, ROOT_DEV - 1).astype(jnp.int32),
        "node_len": place_ends(jax.random.randint(splits[9], (N_REQ, NODES_DEV), 1, NODE_MAX + 1), jax.random.fold_in(splits[9], 1), 1, NODE_MAX).astype(jnp.int32),
        "residual": bell_draw(splits[10], (QUERY_TOKENS, D), 1.0, 6.0, ((0, 16),)),
        "out_proj": bell_draw(splits[11], (QUERY_HEADS * HEAD_SIZE, D), (QUERY_HEADS * HEAD_SIZE) ** -0.5, 0.078125, ((0, 8),)),
        "norm_gain": jnp.clip(1.0 + 0.1 * jax.random.normal(splits[12], (D,), jnp.float32), 0.5, 1.5),
        "gate_proj": bell_draw(splits[13], (D, FF), D ** -0.5, 0.078125, ((1, 128),)),
        "up_proj": bell_draw(splits[14], (D, FF), D ** -0.5, 0.078125, ((1, 128),)),
        "down_proj": bell_draw(splits[15], (FF, D), FF ** -0.5, 0.0546875, ((0, 128),)),
        "next_gain": jnp.clip(1.0 + 0.1 * jax.random.normal(splits[16], (D,), jnp.float32), 0.5, 1.5),
        "qkv_proj": bell_draw(splits[17], (D, QKV), D ** -0.5, 0.078125, ((1, 8),)),
        "qkv_bias": bell_draw(splits[18], (QKV,), 0.5, 3.0, ((0, 8),), jnp.float32),
    }


EPS = 1e-06

def rms_norm(stream, gain):
    values = stream.astype(jnp.float32)
    mean_sq = lax.optimization_barrier(jnp.mean(values * values, axis=-1, keepdims=True))
    return (values * lax.rsqrt(mean_sq + EPS) * gain).astype(jnp.bfloat16)

def attend(queries, leaf_keys, leaf_token_values, prefix_keys, prefix_values, segments, parents, roots, lengths):
    tokens = queries.shape[0]
    heads_kv = leaf_keys.shape[1] // HEAD_SIZE
    query_rows = queries.reshape(tokens, heads_kv, QUERY_PER_KV, HEAD_SIZE).astype(jnp.float32)
    keys = jnp.concatenate([prefix_keys.reshape(-1, heads_kv, HEAD_SIZE), leaf_keys.reshape(tokens, heads_kv, HEAD_SIZE)], 0)
    values = jnp.concatenate([prefix_values.reshape(-1, heads_kv, HEAD_SIZE), leaf_token_values.reshape(tokens, heads_kv, HEAD_SIZE)], 0)
    middle = lax.optimization_barrier(jnp.sum((segments[:, None] == jnp.arange(REQ_DEV)[None, :]) * parents[None, :], axis=1))
    root = lax.optimization_barrier(jnp.sum((middle[:, None] == jnp.arange(MID_DEV)[None, :]) * roots[None, :], axis=1))
    node = jnp.arange(NODES_DEV * NODE_MAX) // NODE_MAX
    inside = (jnp.arange(NODE_MAX)[None, :] < lengths[:, None]).reshape(-1)
    prefix_mask = ((node[None, :] == root[:, None]) | (node[None, :] == ROOT_DEV + middle[:, None])) & inside[None, :]
    place = jnp.arange(tokens)
    leaf_mask = (segments[None, :] == segments[:, None]) & (place[None, :] <= place[:, None])
    mask = jnp.concatenate([prefix_mask, leaf_mask], 1)
    score = jnp.einsum('tkgd,skd->tkgs', query_rows, keys.astype(jnp.float32)) / math.sqrt(HEAD_SIZE)
    score = jnp.where(mask[:, None, None, :], score, -1e+30)
    top = lax.optimization_barrier(jnp.max(score, axis=-1, keepdims=True))
    expo = jnp.where(mask[:, None, None, :], jnp.exp(score - top), 0.0)
    total = lax.optimization_barrier(jnp.sum(expo, axis=-1, keepdims=True))
    weights = expo.astype(jnp.bfloat16)
    summed = jnp.einsum('tkgs,skd->tkgd', weights.astype(jnp.float32), values.astype(jnp.float32))
    return (summed / total).astype(jnp.bfloat16).reshape(tokens, -1)

def reference(queries, leaf_keys, leaf_token_values, key_value_pages, page_holder, page_slot, segment_ids, req_parent, mid_parent, node_len, residual, out_proj, norm_gain, gate_proj, up_proj, down_proj, next_gain, qkv_proj, qkv_bias):
    index = (page_holder * PAGES_PER_GROUP + page_slot).astype(jnp.int32)

    def one_group(group):
        pages = key_value_pages[index[group].reshape(-1)]
        prefix = pages.reshape(NODES_DEV * NODE_MAX, 2, -1)
        start = (group * TOK_GRP).astype(jnp.int32)
        return attend(lax.dynamic_slice_in_dim(queries, start, TOK_GRP, 0), lax.dynamic_slice_in_dim(leaf_keys, start, TOK_GRP, 0), lax.dynamic_slice_in_dim(leaf_token_values, start, TOK_GRP, 0), prefix[:, 0], prefix[:, 1], lax.dynamic_slice_in_dim(segment_ids, start, TOK_GRP, 0), req_parent[group], mid_parent[group], node_len[group])
    attention = lax.map(one_group, jnp.arange(N_REQ, dtype=jnp.int32)).reshape(QUERY_TOKENS, -1)
    projected = jnp.dot(attention, out_proj, preferred_element_type=jnp.float32)
    stream = (residual.astype(jnp.float32) + projected).astype(jnp.bfloat16)
    normed = rms_norm(stream, norm_gain)
    gate = jnp.dot(normed, gate_proj, preferred_element_type=jnp.float32)
    upper = jnp.dot(normed, up_proj, preferred_element_type=jnp.float32)
    hidden = (jax.nn.silu(gate) * upper).astype(jnp.bfloat16)
    mixed = jnp.dot(hidden, down_proj, preferred_element_type=jnp.float32)
    layer_out = (stream.astype(jnp.float32) + mixed).astype(jnp.bfloat16)
    next_normed = rms_norm(layer_out, next_gain)
    qkv_out = (jnp.dot(next_normed, qkv_proj, preferred_element_type=jnp.float32) + qkv_bias).astype(jnp.bfloat16)
    return (layer_out, qkv_out)
```

```python
import functools
import math

import jax
import jax.numpy as jnp
from jax import lax
from jax.experimental import pallas as pl
from jax.experimental.pallas import tpu as pltpu
from jax.sharding import PartitionSpec as P

HEAD_SIZE = 128
QUERY_PER_KV = 5
REQ_DEV = 8
ROOT_DEV = 2
MID_DEV = 4
NODES_DEV = 6
NODE_MAX = 256
MODEL = 5120
ROWS = 16
UNITS = 108
UNITS_PAD = 128
DOWN_PAD = 112
QKV_COLS = 896

EPS = 1e-06

MESH = pl.DeviceIdType.MESH


def attend(
    queries,
    leaf_keys,
    leaf_token_values,
    prefix_keys,
    prefix_values,
    segments,
    parents,
    roots,
    lengths,
):
    tokens = queries.shape[0]
    heads_kv = leaf_keys.shape[1] // HEAD_SIZE
    query_rows = queries.reshape(tokens, heads_kv, QUERY_PER_KV, HEAD_SIZE)
    keys = jnp.concatenate(
        [
            prefix_keys.reshape(-1, heads_kv, HEAD_SIZE),
            leaf_keys.reshape(tokens, heads_kv, HEAD_SIZE),
        ],
        0,
    )
    values = jnp.concatenate(
        [
            prefix_values.reshape(-1, heads_kv, HEAD_SIZE),
            leaf_token_values.reshape(tokens, heads_kv, HEAD_SIZE),
        ],
        0,
    )
    middle = jnp.sum((segments[:, None] == jnp.arange(REQ_DEV)[None, :]) * parents[None, :], axis=1)
    root = jnp.sum((middle[:, None] == jnp.arange(MID_DEV)[None, :]) * roots[None, :], axis=1)
    node = jnp.arange(NODES_DEV * NODE_MAX) // NODE_MAX
    inside = (jnp.arange(NODE_MAX)[None, :] < lengths[:, None]).reshape(-1)
    prefix_mask = (
        (node[None, :] == root[:, None]) | (node[None, :] == ROOT_DEV + middle[:, None])
    ) & inside[None, :]
    place = jnp.arange(tokens)
    leaf_mask = (segments[None, :] == segments[:, None]) & (place[None, :] <= place[:, None])
    mask = jnp.concatenate([prefix_mask, leaf_mask], 1)
    score = jnp.einsum(
        "tkgd,skd->tkgs", query_rows, keys, preferred_element_type=jnp.float32
    ) / math.sqrt(HEAD_SIZE)
    score = jnp.where(mask[:, None, None, :], score, -1e30)
    top = jnp.max(score, axis=-1, keepdims=True)
    expo = jnp.where(mask[:, None, None, :], jnp.exp(score - top), 0.0)
    total = jnp.sum(expo, axis=-1, keepdims=True)
    weights = expo.astype(jnp.bfloat16)
    summed = jnp.einsum("tkgs,skd->tkgd", weights, values, preferred_element_type=jnp.float32)
    return (summed / total).astype(jnp.bfloat16).reshape(tokens, -1)


def fetch_prefix(key_value_pages, page_holder, page_slot):
    groups = lax.axis_size("req")
    myself = lax.axis_index("req")
    holders = page_holder.reshape(groups, -1)
    slots = page_slot.reshape(groups, -1)
    token_count = holders.shape[1]
    room = (token_count // 2 + groups - 2) // (groups - 1)
    earlier = jnp.arange(token_count)[None, :] < jnp.arange(token_count)[:, None]
    same = holders[:, :, None] == holders[:, None, :]
    rank = jnp.sum(same & earlier[None, :, :], axis=-1)
    asked = (holders == myself) & (jnp.arange(groups)[:, None] != myself)
    picked = asked[:, None, :] & (rank[:, None, :] == jnp.arange(room)[None, :, None])
    send_slot = jnp.sum(jnp.where(picked, slots[:, None, :], 0), axis=-1)
    outgoing = key_value_pages[send_slot]
    incoming = lax.all_to_all(outgoing, "req", split_axis=0, concat_axis=0, tiled=True)
    flat_in = incoming.reshape((groups * room,) + incoming.shape[2:])
    own_holders = lax.dynamic_index_in_dim(holders, myself, 0, keepdims=False)
    own_slots = lax.dynamic_index_in_dim(slots, myself, 0, keepdims=False)
    own_rank = lax.dynamic_index_in_dim(rank, myself, 0, keepdims=False)
    remote = flat_in[own_holders * room + jnp.minimum(own_rank, room - 1)]
    local = key_value_pages[own_slots]
    pages = jnp.where((own_holders == myself)[:, None, None, None], local, remote)
    return pages.reshape(NODES_DEV * NODE_MAX, 2, -1)


def place():
    req = lax.axis_index("req")
    mlp = lax.axis_index("mlp")
    return lax.div(mlp, 2), lax.div(req, 4), lax.rem(req, 4), lax.rem(mlp, 2)


def device(x, y, z, core):
    return (y * 4 + z, x * 2 + core)


def ahead(coords, axis, steps):
    moved = list(coords)
    moved[axis] = lax.rem(moved[axis] + steps, 4)
    return moved


def greet(x, y, z, core):
    barrier = pltpu.get_barrier_semaphore()
    others = [device(x, y, z, 1 - core)]
    for axis in range(3):
        for steps in (1, 2, 3):
            others.append(device(*ahead((x, y, z), axis, steps), core))
    for other in others:
        pl.semaphore_signal(barrier, inc=1, device_id=other, device_id_type=MESH)
    pl.semaphore_wait(barrier, len(others))


def remote(src, dst, send, recv, target):
    return pltpu.make_async_remote_copy(
        src_ref=src, dst_ref=dst, send_sem=send, recv_sem=recv, device_id=target, device_id_type=MESH
    )


def normed_rows(rows, gain):
    mean_sq = jnp.mean(rows * rows, axis=-1, keepdims=True)
    return (rows * lax.rsqrt(mean_sq + EPS) * gain).astype(jnp.bfloat16)


PARTS = (
    (0, 1664, (1, 2, 0)),
    (1664, 1664, (2, 0, 1)),
    (3328, 1792, (0, 1, 2)),
)


def spread_kernel(
    projected,
    residual,
    gain,
    weights_hbm,
    stream_out,
    hidden_out,
    resid,
    half,
    summed,
    arrived,
    tokens,
    weights,
    hidden,
    local_sem,
    half_send,
    half_recv,
    sum_send,
    sum_recv,
    weight_sem,
    part_send,
    part_recv,
    hid_send,
    hid_recv,
):
    x, y, z, core = place()
    here = (x, y, z)
    sibling = device(x, y, z, 1 - core)
    own_rows = pl.multiple_of((x * 2 + core) * ROWS, ROWS)
    own_cols = pl.multiple_of(core * 2 * UNITS_PAD, 2 * UNITS_PAD)
    resid_copy = pltpu.make_async_copy(residual.at[pl.ds(own_rows, ROWS), :], resid, local_sem.at[0])
    resid_copy.start()
    weight_copy = pltpu.make_async_copy(
        weights_hbm, weights.at[:, pl.ds(own_cols, 2 * UNITS_PAD)], local_sem.at[1]
    )
    weight_copy.start()
    greet(x, y, z, core)

    halves = []
    for chip in range(4):
        rows = pl.multiple_of((chip * 2 + 1 - core) * ROWS, ROWS)
        copy = remote(
            projected.at[pl.ds(rows, ROWS), :], half.at[chip], half_send.at[chip], half_recv.at[chip], sibling
        )
        copy.start()
        halves.append(copy)
    sums = []
    for steps in (2, 1, 3):
        chip = lax.rem(x + steps, 4)
        rows = pl.multiple_of((chip * 2 + core) * ROWS, ROWS)
        if steps == 2:
            for copy in halves:
                copy.wait_recv()
        summed[steps] = (
            projected[pl.ds(rows, ROWS), :].astype(jnp.float32) + half[chip].astype(jnp.float32)
        ).astype(jnp.bfloat16)
        copy = remote(
            summed.at[steps],
            arrived.at[steps],
            sum_send.at[steps - 1],
            sum_recv.at[steps - 1],
            device(*ahead(here, 0, steps), core),
        )
        copy.start()
        sums.append(copy)
    swap = remote(
        weights_hbm, weights.at[:, pl.ds(own_cols, 2 * UNITS_PAD)], weight_sem.at[0], weight_sem.at[1], sibling
    )
    swap.start()
    total = projected[pl.ds(own_rows, ROWS), :].astype(jnp.float32) + half[x].astype(jnp.float32)
    for copy in sums:
        copy.wait_recv()
    for steps in (1, 2, 3):
        total = total + arrived[steps].astype(jnp.float32)
    resid_copy.wait()
    stream = (resid[...].astype(jnp.float32) + total).astype(jnp.bfloat16)
    stream_out[...] = stream
    tokens[x, y, z] = normed_rows(stream.astype(jnp.float32), gain[...])

    def block(part, phase, coords, first, width):
        order = PARTS[part][2]
        index = list(coords)
        for axis in order[:phase]:
            index[axis] = slice(None)
        return tokens.at[index[0], index[1], index[2], :, pl.ds(first, width)]

    pending = []
    for phase in range(3):
        direct = []
        for part, (first, width, order) in enumerate(PARTS):
            axis = order[phase]
            src = block(part, phase, here, first, width)
            pair = []
            for way, steps in enumerate((1, 3)):
                copy = remote(
                    src,
                    src,
                    part_send.at[part, phase, way],
                    part_recv.at[part, phase, way],
                    device(*ahead(here, axis, steps), core),
                )
                copy.start()
                pair.append(copy)
            direct.append(pair)
        onward = []
        for part, (first, width, order) in enumerate(PARTS):
            axis = order[phase]
            cut = 896
            for way, (steps, start, size) in enumerate(((1, first, cut), (3, first + cut, width - cut))):
                direct[part][way].wait_recv()
                src = block(part, phase, ahead(here, axis, 4 - steps), start, size)
                copy = remote(
                    src,
                    src,
                    part_send.at[part, phase, 2 + way],
                    part_recv.at[part, phase, 2 + way],
                    device(*ahead(here, axis, steps), core),
                )
                copy.start()
                onward.append(copy)
        for copy in onward:
            copy.wait_recv()
        pending += [copy for pair in direct for copy in pair] + onward

    weight_copy.wait()
    swap.wait_recv()

    @pl.loop(0, 4)
    def _(step):
        chip = lax.rem(x + 3 - step, 4)
        for line in range(4):
            rows = tokens[chip, line].reshape(4 * ROWS, MODEL)
            both = jnp.dot(rows, weights[...], preferred_element_type=jnp.float32)
            outs = []
            for which in range(2):
                gate = both[:, which * 2 * UNITS_PAD : which * 2 * UNITS_PAD + UNITS_PAD]
                upper = both[:, which * 2 * UNITS_PAD + UNITS_PAD : (which + 1) * 2 * UNITS_PAD]
                outs.append((gate / (1.0 + jnp.exp(-gate)) * upper).astype(jnp.bfloat16))
            hidden[chip, pl.ds(line * 4 * ROWS, 4 * ROWS), :] = jnp.concatenate(outs, axis=1)

    spot = hidden_out.at[:, pl.ds(pl.multiple_of(x * 2 * UNITS_PAD, 2 * UNITS_PAD), 2 * UNITS_PAD)]
    for steps in (2, 1, 3):
        target = ahead(here, 0, steps)
        copy = remote(
            hidden.at[target[0]], spot, hid_send.at[steps - 1], hid_recv.at[steps - 1], device(*target, core)
        )
        copy.start()
        pending.append(copy)
        copy_list = copy
        sums.append(copy_list)
    own_hidden = pltpu.make_async_copy(hidden.at[x], spot, local_sem.at[2])
    own_hidden.start()
    own_hidden.wait()
    for copy in sums[3:]:
        copy.wait_recv()
    for copy in halves + sums[:3] + [swap] + pending:
        copy.wait_send()


def spread(projected, residual, gain, weights):
    vmem = pl.BlockSpec(memory_space=pltpu.VMEM)
    anywhere = pl.BlockSpec(memory_space=pl.ANY)
    return pl.pallas_call(
        spread_kernel,
        out_shape=(
            jax.ShapeDtypeStruct((ROWS, MODEL), jnp.bfloat16),
            jax.ShapeDtypeStruct((256, 8 * UNITS_PAD), jnp.bfloat16),
        ),
        in_specs=[vmem, anywhere, vmem, anywhere],
        out_specs=(vmem, anywhere),
        scratch_shapes=[
            pltpu.VMEM((ROWS, MODEL), jnp.bfloat16),
            pltpu.VMEM((4, ROWS, MODEL), jnp.bfloat16),
            pltpu.VMEM((4, ROWS, MODEL), jnp.bfloat16),
            pltpu.VMEM((4, ROWS, MODEL), jnp.bfloat16),
            pltpu.VMEM((4, 4, 4, ROWS, MODEL), jnp.bfloat16),
            pltpu.VMEM((MODEL, 4 * UNITS_PAD), jnp.bfloat16),
            pltpu.VMEM((4, 256, 2 * UNITS_PAD), jnp.bfloat16),
            pltpu.SemaphoreType.DMA((3,)),
            pltpu.SemaphoreType.DMA((4,)),
            pltpu.SemaphoreType.DMA((4,)),
            pltpu.SemaphoreType.DMA((3,)),
            pltpu.SemaphoreType.DMA((3,)),
            pltpu.SemaphoreType.DMA((2,)),
            pltpu.SemaphoreType.DMA((3, 3, 4)),
            pltpu.SemaphoreType.DMA((3, 3, 4)),
            pltpu.SemaphoreType.DMA((3,)),
            pltpu.SemaphoreType.DMA((3,)),
        ],
        compiler_params=pltpu.CompilerParams(
            collective_id=0, has_side_effects=True, vmem_limit_bytes=48 << 20
        ),
        cost_estimate=pl.CostEstimate(flops=2 * 1024 * 5120 * 512, bytes_accessed=200 << 20, transcendentals=0),
    )(projected, residual, gain, weights)


CHUNKS = 4


def gather_kernel(
    hidden_hbm,
    down_hbm,
    stream,
    gain,
    qkv_hbm,
    bias,
    layer_out,
    qkv_out,
    hidden,
    down,
    qkv,
    partial,
    first_in,
    second,
    second_in,
    rows,
    local_sem,
    down_sem,
    first_send,
    first_recv,
    second_send,
    second_recv,
    row_send,
    row_recv,
):
    x, y, z, core = place()
    here = (x, y, z)
    sibling = device(x, y, z, 1 - core)
    hidden_copy = pltpu.make_async_copy(hidden_hbm, hidden, local_sem.at[0])
    hidden_copy.start()
    down_copies = []
    for member in range(8):
        copy = pltpu.make_async_copy(
            down_hbm.at[member], down.at[member, pl.ds(0, DOWN_PAD), :], down_sem.at[member]
        )
        copy.start()
        down_copies.append(copy)
    qkv_copy = pltpu.make_async_copy(qkv_hbm, qkv, local_sem.at[1])
    qkv_copy.start()
    for member in range(8):
        down[member, pl.ds(DOWN_PAD, UNITS_PAD - DOWN_PAD), :] = jnp.zeros(
            (UNITS_PAD - DOWN_PAD, MODEL), jnp.bfloat16
        )
    greet(x, y, z, core)
    hidden_copy.wait()
    for copy in down_copies:
        copy.wait()

    size = MODEL // CHUNKS
    sent = []
    firsts = []
    for chunk in range(CHUNKS):
        cols = pl.ds(chunk * size, size)
        total = jnp.dot(
            hidden[...],
            down[:, :, chunk * size : (chunk + 1) * size].reshape(8 * UNITS_PAD, size),
            preferred_element_type=jnp.float32,
        )
        partial[:, :, :, cols] = total.astype(jnp.bfloat16).reshape(4, 4, ROWS, size)
        axis = 1 + chunk % 2
        copies = []
        for steps in (2, 1, 3):
            target = ahead(here, axis, steps)
            src = partial.at[target[1], :, :, cols] if axis == 1 else partial.at[:, target[2], :, cols]
            copy = remote(
                src,
                first_in.at[chunk, steps - 1],
                first_send.at[chunk, steps - 1],
                first_recv.at[chunk, steps - 1],
                device(*target, core),
            )
            copy.start()
            copies.append(copy)
        firsts.append(copies)
        sent += copies
    seconds = []
    for chunk in range(CHUNKS):
        cols = pl.ds(chunk * size, size)
        axis = 1 + chunk % 2
        for copy in firsts[chunk]:
            copy.wait_recv()
        own = partial[y, :, :, cols] if axis == 1 else partial[:, z, :, cols]
        total = own.astype(jnp.float32)
        for steps in range(3):
            total = total + first_in[chunk, steps].astype(jnp.float32)
        second[chunk] = total.astype(jnp.bfloat16)
        copies = []
        for steps in (2, 1, 3):
            target = ahead(here, 3 - axis, steps)
            copy = remote(
                second.at[chunk, target[3 - axis]],
                second_in.at[chunk, steps - 1],
                second_send.at[chunk, steps - 1],
                second_recv.at[chunk, steps - 1],
                device(*target, core),
            )
            copy.start()
            copies.append(copy)
        seconds.append(copies)
        sent += copies
    parts = []
    for chunk in range(CHUNKS):
        axis = 1 + chunk % 2
        for copy in seconds[chunk]:
            copy.wait_recv()
        total = second[chunk, here[3 - axis]].astype(jnp.float32)
        for steps in range(3):
            total = total + second_in[chunk, steps].astype(jnp.float32)
        parts.append(total)
    mixed = jnp.concatenate(parts, axis=1)
    out = (stream[...].astype(jnp.float32) + mixed).astype(jnp.bfloat16)
    layer_out[...] = out
    mine = x * 2 + core
    rows[mine] = normed_rows(out.astype(jnp.float32), gain[...])
    ring = []
    for steps in (2, 1, 3):
        copy = remote(
            rows.at[mine],
            rows.at[mine],
            row_send.at[steps - 1],
            row_recv.at[steps - 1],
            device(*ahead(here, 0, steps), core),
        )
        copy.start()
        ring.append((steps, copy))
    twins = []
    copy = remote(rows.at[mine], rows.at[mine], row_send.at[3], row_recv.at[3], sibling)
    copy.start()
    twins.append(copy)
    for steps, arrival in reversed(ring):
        arrival.wait_recv()
        other = lax.rem(x + 4 - steps, 4) * 2 + core
        copy = remote(rows.at[other], rows.at[other], row_send.at[3 + steps], row_recv.at[3 + steps], sibling)
        copy.start()
        twins.append(copy)
    for copy in twins:
        copy.wait_recv()
    qkv_copy.wait()
    result = jnp.dot(rows[...].reshape(8 * ROWS, MODEL), qkv[...], preferred_element_type=jnp.float32)
    qkv_out[...] = (result + bias[...]).astype(jnp.bfloat16)
    for copy in sent + [copy for _, copy in ring] + twins:
        copy.wait_send()


def gather(hidden, down, stream, gain, qkv, bias):
    vmem = pl.BlockSpec(memory_space=pltpu.VMEM)
    anywhere = pl.BlockSpec(memory_space=pl.ANY)
    size = MODEL // CHUNKS
    return pl.pallas_call(
        gather_kernel,
        out_shape=(
            jax.ShapeDtypeStruct((ROWS, MODEL), jnp.bfloat16),
            jax.ShapeDtypeStruct((8 * ROWS, QKV_COLS), jnp.bfloat16),
        ),
        in_specs=[anywhere, anywhere, vmem, vmem, anywhere, vmem],
        out_specs=(vmem, vmem),
        scratch_shapes=[
            pltpu.VMEM((256, 8 * UNITS_PAD), jnp.bfloat16),
            pltpu.VMEM((8, UNITS_PAD, MODEL), jnp.bfloat16),
            pltpu.VMEM((MODEL, QKV_COLS), jnp.bfloat16),
            pltpu.VMEM((4, 4, ROWS, MODEL), jnp.bfloat16),
            pltpu.VMEM((CHUNKS, 3, 4, ROWS, size), jnp.bfloat16),
            pltpu.VMEM((CHUNKS, 4, ROWS, size), jnp.bfloat16),
            pltpu.VMEM((CHUNKS, 3, ROWS, size), jnp.bfloat16),
            pltpu.VMEM((8, ROWS, MODEL), jnp.bfloat16),
            pltpu.SemaphoreType.DMA((2,)),
            pltpu.SemaphoreType.DMA((8,)),
            pltpu.SemaphoreType.DMA((CHUNKS, 3)),
            pltpu.SemaphoreType.DMA((CHUNKS, 3)),
            pltpu.SemaphoreType.DMA((CHUNKS, 3)),
            pltpu.SemaphoreType.DMA((CHUNKS, 3)),
            pltpu.SemaphoreType.DMA((7,)),
            pltpu.SemaphoreType.DMA((7,)),
        ],
        compiler_params=pltpu.CompilerParams(
            collective_id=1, has_side_effects=True, vmem_limit_bytes=48 << 20
        ),
        cost_estimate=pl.CostEstimate(flops=2 * 256 * 5120 * 1024, bytes_accessed=100 << 20, transcendentals=0),
    )(hidden, down, stream, gain, qkv, bias)


def body(
    queries,
    leaf_keys,
    leaf_token_values,
    key_value_pages,
    page_holder,
    page_slot,
    segment_ids,
    req_parent,
    mid_parent,
    node_len,
    residual,
    out_proj,
    norm_gain,
    gate_proj,
    up_proj,
    down_proj,
    next_gain,
    qkv_proj,
    qkv_bias,
):
    down_padded = jnp.pad(down_proj, ((0, DOWN_PAD - UNITS), (0, 0)))
    down_all = lax.all_gather(down_padded, "mlp", axis=0, tiled=False)
    lanes = ((0, 0), (0, UNITS_PAD - UNITS))
    weights = jnp.concatenate([jnp.pad(gate_proj, lanes), jnp.pad(up_proj, lanes)], axis=1)
    prefix = fetch_prefix(key_value_pages, page_holder, page_slot)
    attention = attend(
        queries,
        leaf_keys,
        leaf_token_values,
        prefix[:, 0],
        prefix[:, 1],
        segment_ids,
        req_parent[0],
        mid_parent[0],
        node_len[0],
    )
    projected = jnp.dot(attention, out_proj, preferred_element_type=jnp.float32).astype(jnp.bfloat16)
    stream, hidden = spread(projected, residual, norm_gain.reshape(1, -1), weights)
    return gather(hidden, down_all, stream, next_gain.reshape(1, -1), qkv_proj, qkv_bias.reshape(1, -1))


def solution(mesh):
    placed = (
        P("req", "mlp"),
        P("req", "mlp"),
        P("req", "mlp"),
        P("req", None, None, "mlp"),
        P(),
        P(),
        P("req"),
        P("req", None),
        P("req", None),
        P("req", None),
        P("req", None),
        P("mlp", None),
        P(),
        P(None, ("req", "mlp")),
        P(None, ("req", "mlp")),
        P(("req", "mlp"), None),
        P(),
        P(None, "mlp"),
        P("mlp"),
    )
    return jax.shard_map(
        body,
        mesh=mesh,
        in_specs=placed,
        out_specs=(P(("req", "mlp"), None), P("req", "mlp")),
        check_vma=False,
    )
```

```python
import functools
import math

import jax
import jax.numpy as jnp
from jax import lax
from jax.experimental import pallas as pl
from jax.experimental.pallas import tpu as pltpu
from jax.sharding import PartitionSpec as P

HEAD_SIZE = 128
QUERY_PER_KV = 5
REQ_DEV = 8
ROOT_DEV = 2
MID_DEV = 4
NODES_DEV = 6
NODE_MAX = 256
MODEL = 5120
ROWS = 16
UNITS = 108
UNITS_PAD = 128
DOWN_PAD = 112
QKV_COLS = 896
TOKENS = 128
PAGES = 32
PAGE = 64
ENTRIES = 24
PREFIX = NODES_DEV * NODE_MAX
SLICES = 4
CHUNKS = 4
HIDDEN = -1e30

EPS = 1e-06

MESH = pl.DeviceIdType.MESH


def place():
    req = lax.axis_index("req")
    mlp = lax.axis_index("mlp")
    return lax.div(mlp, 2), lax.div(req, 4), lax.rem(req, 4), lax.rem(mlp, 2)


def device(x, y, z, core):
    return (y * 4 + z, x * 2 + core)


def ahead(coords, axis, steps):
    moved = list(coords)
    moved[axis] = lax.rem(moved[axis] + steps, 4)
    return moved


def greet(others):
    barrier = pltpu.get_barrier_semaphore()
    for other in others:
        pl.semaphore_signal(barrier, inc=1, device_id=other, device_id_type=MESH)


def greeted(others):
    pl.semaphore_wait(pltpu.get_barrier_semaphore(), len(others))


def lines_through(x, y, z, core):
    others = [device(x, y, z, 1 - core)]
    for axis in range(3):
        for steps in (1, 2, 3):
            others.append(device(*ahead((x, y, z), axis, steps), core))
    return others


def remote(src, dst, send, recv, target):
    return pltpu.make_async_remote_copy(
        src_ref=src, dst_ref=dst, send_sem=send, recv_sem=recv, device_id=target, device_id_type=MESH
    )


def normed_rows(rows, gain):
    mean_sq = jnp.mean(rows * rows, axis=-1, keepdims=True)
    return (rows * lax.rsqrt(mean_sq + EPS) * gain).astype(jnp.bfloat16)


PARTS = (
    (0, 640, 256, (1, 2, 0)),
    (640, 2048, 1024, (2, 0, 1)),
    (2688, 2432, 1280, (0, 1, 2)),
)


def layer_kernel(
    queries,
    leaf_keys,
    leaf_values,
    pages_hbm,
    holder,
    slot,
    segment_row,
    req_parent,
    mid_parent,
    node_len,
    residual,
    out_hbm,
    gain,
    gate_hbm,
    up_hbm,
    down_hbm,
    next_gain,
    qkv_hbm,
    bias,
    layer_out,
    qkv_out,
    pages,
    outgoing,
    incoming,
    keys,
    values,
    hide,
    attention,
    out_proj,
    gate_up,
    own_down,
    projected,
    resid,
    half,
    summed,
    arrived,
    tokens,
    weights,
    hidden,
    hidden_in,
    sums_f32,
    down,
    qkv,
    first_in,
    second,
    second_in,
    rows,
    local_sem,
    page_send,
    page_recv,
    half_send,
    half_recv,
    sum_send,
    sum_recv,
    weight_sem,
    part_send,
    part_recv,
    hid_send,
    hid_recv,
    down_send,
    down_recv,
    twin_send,
    twin_recv,
    first_send,
    first_recv,
    second_send,
    second_recv,
    row_send,
    row_recv,
):
    x, y, z, core = place()
    here = (x, y, z)
    group = lax.axis_index("req")
    sibling = device(x, y, z, 1 - core)
    own_rows = pl.multiple_of((x * 2 + core) * ROWS, ROWS)
    own_cols = pl.multiple_of(core * 2 * UNITS_PAD, 2 * UNITS_PAD)
    mine = x * 2 + core
    others = lines_through(x, y, z, core)
    plane = []
    for offset in range(1, 16):
        spot = (x, lax.rem(y + offset // 4, 4), lax.rem(z + offset % 4, 4))
        plane.append(spot)
        if offset // 4 and offset % 4:
            others.append(device(*spot, core))
    greet(others)

    def local(src, dst, index):
        copy = pltpu.make_async_copy(src, dst, local_sem.at[index])
        copy.start()
        return copy

    pages_copy = local(pages_hbm, pages, 0)
    gate_copy = local(gate_hbm, gate_up.at[0], 1)
    up_copy = local(up_hbm, gate_up.at[1], 2)
    down_copy = local(down_hbm, own_down, 5)
    out_copy = local(out_hbm, out_proj, 3)
    resid_copy = local(residual.at[pl.ds(own_rows, ROWS), :], resid, 4)
    qkv_copy = local(qkv_hbm, qkv, 6)

    pages_copy.wait()
    for number, spot in enumerate(plane):
        asker = spot[1] * 4 + spot[2]
        picked = jnp.int32(0)
        for entry in range(ENTRIES):
            picked = jnp.where(holder[entry // 4, entry % 4, asker] == group, slot[entry // 4, entry % 4, asker], picked)
        outgoing[number] = pages[picked]
    greeted(others)
    fetched = []
    for number in range(14, -1, -1):
        copy = remote(
            outgoing.at[number],
            incoming.at[group],
            page_send.at[number],
            page_recv.at[number],
            device(*plane[number], core),
        )
        copy.start()
        fetched.append(copy)

    gate_copy.wait()
    up_copy.wait()
    for which in range(2):
        cols = pl.ds(pl.multiple_of(own_cols + which * UNITS_PAD, UNITS_PAD), UNITS_PAD)
        weights[:, cols] = jnp.concatenate(
            [gate_up[which], jnp.zeros((UNITS_PAD - UNITS, MODEL), jnp.bfloat16)], axis=0
        ).T
    spot = weights.at[:, pl.ds(own_cols, 2 * UNITS_PAD)]
    swap = remote(spot, spot, weight_sem.at[0], weight_sem.at[1], sibling)
    swap.start()

    twins = []
    downs = []

    def down_block(offset, first, width):
        member = lax.rem(x + offset, 4) * 2 + core
        return down.at[member, pl.ds(0, DOWN_PAD), pl.ds(first, width)]

    def down_push(kind, part, way, offset, first, width):
        view = down_block(offset, first, width)
        copy = remote(
            view,
            view,
            down_send.at[kind, part, way],
            down_recv.at[kind, part, way],
            device(*ahead(here, 0, (1, 3)[way]), core),
        )
        copy.start()
        downs.append(copy)
        return copy

    def twin(offset):
        view = down_block(offset, 0, MODEL)
        copy = remote(view, view, twin_send.at[offset], twin_recv.at[offset], sibling)
        copy.start()
        twins.append(copy)

    wide = MODEL // 2

    def down_direct(part):
        return [down_push(0, part, way, 0, part * wide, wide) for way in range(2)]

    def down_onward(part):
        return [
            down_push(1, part, way, behind, part * wide + way * (wide // 2), wide // 2)
            for way, behind in enumerate((3, 1))
        ]

    down_copy.wait()
    down[mine, pl.ds(0, DOWN_PAD), :] = jnp.concatenate(
        [own_down[...], jnp.zeros((DOWN_PAD - UNITS, MODEL), jnp.bfloat16)], axis=0
    )
    for member in range(8):
        down[member, pl.ds(DOWN_PAD, UNITS_PAD - DOWN_PAD), :] = jnp.zeros(
            (UNITS_PAD - DOWN_PAD, MODEL), jnp.bfloat16
        )
    down_near = [down_direct(0)]
    twin(0)

    line = segment_row[...]
    across = lax.broadcasted_iota(jnp.int32, (TOKENS, TOKENS), 1)
    along = lax.broadcasted_iota(jnp.int32, (TOKENS, TOKENS), 0)
    segments = jnp.sum(jnp.where(across == along, line, 0), axis=1, keepdims=True)
    middle = jnp.zeros_like(segments)
    for request in range(REQ_DEV):
        middle = jnp.where(segments == request, req_parent[0, request], middle)
    root = jnp.zeros_like(segments)
    for node in range(MID_DEV):
        root = jnp.where(middle == node, mid_parent[0, node], root)
    position = lax.broadcasted_iota(jnp.int32, (TOKENS, NODE_MAX), 1)
    for node in range(NODES_DEV):
        chosen = root == node if node < ROOT_DEV else middle == node - ROOT_DEV
        length = jnp.where(chosen, node_len[0, node], 0)
        hide[:, node * NODE_MAX : (node + 1) * NODE_MAX] = jnp.where(position < length, 0.0, HIDDEN)
    hide[:, PREFIX:] = jnp.where((segments == line) & (across <= along), 0.0, HIDDEN)

    for copy in fetched:
        copy.wait_recv()
    for entry in range(ENTRIES):
        kept = holder[entry // 4, entry % 4, group]
        page = jnp.where(kept == group, pages[slot[entry // 4, entry % 4, group]], incoming[kept])
        keys[entry * PAGE : (entry + 1) * PAGE, :] = page[:, :HEAD_SIZE]
        values[entry * PAGE : (entry + 1) * PAGE, :] = page[:, HEAD_SIZE:]
    keys[PREFIX:, :] = leaf_keys[...]
    values[PREFIX:, :] = leaf_values[...]
    for head in range(QUERY_PER_KV):
        cols = slice(head * HEAD_SIZE, (head + 1) * HEAD_SIZE)
        score = lax.dot_general(
            queries[:, cols], keys[...], (((1,), (1,)), ((), ())), preferred_element_type=jnp.float32
        )
        score = score * (1.0 / math.sqrt(HEAD_SIZE)) + hide[...]
        expo = jnp.exp(score - jnp.max(score, axis=1, keepdims=True))
        total = jnp.sum(expo, axis=1, keepdims=True)
        seen = jnp.dot(expo.astype(jnp.bfloat16), values[...], preferred_element_type=jnp.float32)
        attention[:, cols] = (seen / total).astype(jnp.bfloat16)

    out_copy.wait()
    size = MODEL // SLICES
    halves = []
    for piece in range(SLICES):
        cols = slice(piece * size, (piece + 1) * size)
        term = jnp.dot(attention[...], out_proj[:, cols], preferred_element_type=jnp.float32)
        term = term.astype(jnp.bfloat16).reshape(4, 2, ROWS, size)
        projected[0, :, :, cols] = term[:, 0]
        projected[1, :, :, cols] = term[:, 1]
        copy = remote(
            projected.at[1 - core, :, :, cols],
            half.at[:, :, cols],
            half_send.at[piece],
            half_recv.at[piece],
            sibling,
        )
        copy.start()
        halves.append(copy)
    sums = []
    for piece in range(SLICES):
        cols = slice(piece * size, (piece + 1) * size)
        halves[piece].wait_recv()
        for steps in (2, 1, 3):
            chip = lax.rem(x + steps, 4)
            summed[steps, :, cols] = (
                projected[core, chip, :, cols].astype(jnp.float32) + half[chip, :, cols].astype(jnp.float32)
            ).astype(jnp.bfloat16)
            copy = remote(
                summed.at[steps, :, cols],
                arrived.at[steps, :, cols],
                sum_send.at[piece, steps - 1],
                sum_recv.at[piece, steps - 1],
                device(*ahead(here, 0, steps), core),
            )
            copy.start()
            sums.append(copy)
    total = projected[core, x].astype(jnp.float32) + half[x].astype(jnp.float32)
    down_far = []
    for copy in down_near[0]:
        copy.wait_recv()
    down_far += down_onward(0)
    for copy in sums:
        copy.wait_recv()
    for steps in (1, 2, 3):
        total = total + arrived[steps].astype(jnp.float32)
    resid_copy.wait()
    stream = (resid[...].astype(jnp.float32) + total).astype(jnp.bfloat16)
    tokens[x, y, z] = normed_rows(stream.astype(jnp.float32), gain[...])

    def block(part, offsets, half=None):
        first, width, cut, order = PARTS[part]
        if half is not None:
            first, width = ((first, cut), (first + cut, width - cut))[half]
        index = [slice(None)] * 3
        for axis, offset in zip(order, offsets):
            if offset is not None:
                index[axis] = lax.rem(here[axis] + offset, 4)
        return (index[0], index[1], index[2], slice(None), pl.ds(first, width))

    pending = []

    def push(part, phase, slot, way, spot):
        view = tokens.at[spot]
        copy = remote(
            view,
            view,
            part_send.at[part, phase, slot, way],
            part_recv.at[part, phase, slot, way],
            device(*ahead(here, PARTS[part][3][phase], (1, 3)[way]), core),
        )
        copy.start()
        pending.append(copy)
        return copy

    def both_ways(part, phase, slot, offsets):
        spot = block(part, offsets)
        return [push(part, phase, slot, way, spot) for way in range(2)]

    def onward(part, phase, slot, offsets):
        return [
            push(part, phase, slot, way, block(part, offsets[:phase] + (behind,) + offsets[phase + 1 :], way))
            for way, behind in enumerate((3, 1))
        ]

    def arrive(copies):
        for copy in copies:
            copy.wait_recv()

    def product(part, offset):
        first, width, _, order = PARTS[part]
        index = [slice(None)] * 3
        index[order[2]] = lax.rem(here[order[2]] + offset, 4)
        rows = tokens[index[0], index[1], index[2], :, pl.ds(first, width)].reshape(256, width)
        term = jnp.dot(rows, weights[pl.ds(first, width), :], preferred_element_type=jnp.float32)
        spot = (index[0], index[1], index[2])
        shape = [4, 4, 4]
        del shape[order[2]]
        sums_f32[spot] += term.reshape(*shape, ROWS, 4 * UNITS_PAD)

    every = range(3)
    near = [both_ways(part, 0, 0, (0, 0, 0)) for part in every]
    lines = [both_ways(part, 1, 0, (0, 0, 0)) for part in every]
    down_near.append(down_direct(1))
    sums_f32[...] = jnp.zeros_like(sums_f32)
    far = []
    for part in every:
        arrive(near[part])
        far.append(onward(part, 0, 1, (0, 0, 0)))
        for slot, offset in ((1, 1), (2, 3)):
            lines[part] += both_ways(part, 1, slot, (offset, 0, 0))
    planes = [[None] * 4 for _ in every]
    for part in every:
        arrive(far[part])
        lines[part] += both_ways(part, 1, 3, (2, 0, 0))
        planes[part][0] = both_ways(part, 2, 0, (None, 0, 0))
    far = []
    for part in every:
        arrive(lines[part])
        far.append(onward(part, 1, 4, (None, 0, 0)))
        for offset in (1, 3):
            planes[part][offset] = both_ways(part, 2, offset, (None, offset, 0))
    for part in every:
        arrive(far[part])
        planes[part][2] = both_ways(part, 2, 2, (None, 2, 0))
    swap.wait_recv()
    arrive(down_near[1])
    down_far += down_onward(1)
    twin(1)
    twin(3)
    last = []
    for offset in (0, 1, 3, 2):
        for part in every:
            arrive(planes[part][offset])
            last += onward(part, 2, 4 + offset, (None, offset, 0))
        if offset in (0, 1, 3):
            product((0, 1, None, 2)[offset], 0)
    for part in every:
        product(part, 1)
        product(part, 3)
    arrive(down_far)
    twin(2)
    arrive(last)
    for part in every:
        product(part, 2)

    given = []
    spot = hidden_in.at[:, pl.ds(pl.multiple_of(x * 2 * UNITS_PAD, 2 * UNITS_PAD), 2 * UNITS_PAD)]
    for steps in (2, 1, 3, 0):
        target = ahead(here, 0, steps)
        chip = target[0]
        both = sums_f32[chip].reshape(256, 4 * UNITS_PAD)
        outs = []
        for which in range(2):
            gate = both[:, which * 2 * UNITS_PAD : which * 2 * UNITS_PAD + UNITS_PAD]
            upper = both[:, which * 2 * UNITS_PAD + UNITS_PAD : (which + 1) * 2 * UNITS_PAD]
            outs.append((gate / (1.0 + jnp.exp(-gate)) * upper).astype(jnp.bfloat16))
        if steps:
            hidden[steps - 1] = jnp.concatenate(outs, axis=1)
            copy = remote(
                hidden.at[steps - 1], spot, hid_send.at[steps - 1], hid_recv.at[steps - 1], device(*target, core)
            )
            copy.start()
            given.append(copy)
        else:
            spot[...] = jnp.concatenate(outs, axis=1)
    for copy in pending:
        copy.wait_send()
    partial = tokens.at[0]
    arrive(given)
    arrive(twins)

    size = MODEL // CHUNKS
    sent = []
    firsts = []
    for chunk in range(CHUNKS):
        cols = pl.ds(chunk * size, size)
        total = jnp.dot(
            hidden_in[...],
            down[:, :, chunk * size : (chunk + 1) * size].reshape(8 * UNITS_PAD, size),
            preferred_element_type=jnp.float32,
        )
        partial[:, :, :, cols] = total.astype(jnp.bfloat16).reshape(4, 4, ROWS, size)
        axis = 1 + chunk % 2
        copies = []
        for steps in (2, 1, 3):
            target = ahead(here, axis, steps)
            src = partial.at[target[1], :, :, cols] if axis == 1 else partial.at[:, target[2], :, cols]
            copy = remote(
                src,
                first_in.at[chunk, steps - 1],
                first_send.at[chunk, steps - 1],
                first_recv.at[chunk, steps - 1],
                device(*target, core),
            )
            copy.start()
            copies.append(copy)
        firsts.append(copies)
        sent += copies
    seconds = []
    for chunk in range(CHUNKS):
        cols = pl.ds(chunk * size, size)
        axis = 1 + chunk % 2
        for copy in firsts[chunk]:
            copy.wait_recv()
        own = partial[y, :, :, cols] if axis == 1 else partial[:, z, :, cols]
        total = own.astype(jnp.float32)
        for steps in range(3):
            total = total + first_in[chunk, steps].astype(jnp.float32)
        second[chunk] = total.astype(jnp.bfloat16)
        copies = []
        for steps in (2, 1, 3):
            target = ahead(here, 3 - axis, steps)
            copy = remote(
                second.at[chunk, target[3 - axis]],
                second_in.at[chunk, steps - 1],
                second_send.at[chunk, steps - 1],
                second_recv.at[chunk, steps - 1],
                device(*target, core),
            )
            copy.start()
            copies.append(copy)
        seconds.append(copies)
        sent += copies
    parts = []
    for chunk in range(CHUNKS):
        axis = 1 + chunk % 2
        for copy in seconds[chunk]:
            copy.wait_recv()
        total = second[chunk, here[3 - axis]].astype(jnp.float32)
        for steps in range(3):
            total = total + second_in[chunk, steps].astype(jnp.float32)
        parts.append(total)
    mixed = jnp.concatenate(parts, axis=1)
    out = (stream.astype(jnp.float32) + mixed).astype(jnp.bfloat16)
    layer_out[...] = out
    rows[mine] = normed_rows(out.astype(jnp.float32), next_gain[...])
    ring = []
    for steps in (2, 1, 3):
        copy = remote(
            rows.at[mine],
            rows.at[mine],
            row_send.at[steps - 1],
            row_recv.at[steps - 1],
            device(*ahead(here, 0, steps), core),
        )
        copy.start()
        ring.append((steps, copy))
    passed = []
    copy = remote(rows.at[mine], rows.at[mine], row_send.at[3], row_recv.at[3], sibling)
    copy.start()
    passed.append(copy)
    for steps, arrival in reversed(ring):
        arrival.wait_recv()
        other = lax.rem(x + 4 - steps, 4) * 2 + core
        copy = remote(rows.at[other], rows.at[other], row_send.at[3 + steps], row_recv.at[3 + steps], sibling)
        copy.start()
        passed.append(copy)
    for copy in passed:
        copy.wait_recv()
    qkv_copy.wait()
    result = jnp.dot(rows[...].reshape(8 * ROWS, MODEL), qkv[...], preferred_element_type=jnp.float32)
    qkv_out[...] = (result + bias[...]).astype(jnp.bfloat16)
    for copy in fetched + halves + sums + [swap] + downs + twins + given + sent + [copy for _, copy in ring] + passed:
        copy.wait_send()


def layer(*operands):
    vmem = pl.BlockSpec(memory_space=pltpu.VMEM)
    smem = pl.BlockSpec(memory_space=pltpu.SMEM)
    anywhere = pl.BlockSpec(memory_space=pl.ANY)
    dma = pltpu.SemaphoreType.DMA

    def held(*shape):
        return pltpu.VMEM(shape, jnp.bfloat16)

    size = MODEL // CHUNKS
    return pl.pallas_call(
        layer_kernel,
        out_shape=(
            jax.ShapeDtypeStruct((ROWS, MODEL), jnp.bfloat16),
            jax.ShapeDtypeStruct((TOKENS, QKV_COLS), jnp.bfloat16),
        ),
        in_specs=[vmem] * 3
        + [anywhere, smem, smem, vmem, smem, smem, smem, anywhere, anywhere, vmem]
        + [anywhere, anywhere, anywhere, vmem, anywhere, vmem],
        out_specs=(vmem, vmem),
        scratch_shapes=[
            held(PAGES, PAGE, 2 * HEAD_SIZE),
            held(15, PAGE, 2 * HEAD_SIZE),
            held(16, PAGE, 2 * HEAD_SIZE),
            held(PREFIX + TOKENS, HEAD_SIZE),
            held(PREFIX + TOKENS, HEAD_SIZE),
            pltpu.VMEM((TOKENS, PREFIX + TOKENS), jnp.float32),
            held(TOKENS, QUERY_PER_KV * HEAD_SIZE),
            held(QUERY_PER_KV * HEAD_SIZE, MODEL),
            held(2, UNITS, MODEL),
            held(UNITS, MODEL),
            held(2, 4, ROWS, MODEL),
            held(ROWS, MODEL),
            held(4, ROWS, MODEL),
            held(4, ROWS, MODEL),
            held(4, ROWS, MODEL),
            held(4, 4, 4, ROWS, MODEL),
            held(MODEL, 4 * UNITS_PAD),
            held(3, 256, 2 * UNITS_PAD),
            held(256, 8 * UNITS_PAD),
            pltpu.VMEM((4, 4, 4, ROWS, 4 * UNITS_PAD), jnp.float32),
            held(8, UNITS_PAD, MODEL),
            held(MODEL, QKV_COLS),
            held(CHUNKS, 3, 4, ROWS, size),
            held(CHUNKS, 4, ROWS, size),
            held(CHUNKS, 3, ROWS, size),
            held(8, ROWS, MODEL),
            dma((7,)),
            dma((15,)),
            dma((15,)),
            dma((SLICES,)),
            dma((SLICES,)),
            dma((SLICES, 3)),
            dma((SLICES, 3)),
            dma((2,)),
            dma((3, 3, 8, 2)),
            dma((3, 3, 8, 2)),
            dma((3,)),
            dma((3,)),
            dma((2, 2, 2)),
            dma((2, 2, 2)),
            dma((4,)),
            dma((4,)),
            dma((CHUNKS, 3)),
            dma((CHUNKS, 3)),
            dma((CHUNKS, 3)),
            dma((CHUNKS, 3)),
            dma((7,)),
            dma((7,)),
        ],
        compiler_params=pltpu.CompilerParams(
            collective_id=0, has_side_effects=True, vmem_limit_bytes=63 << 20
        ),
        cost_estimate=pl.CostEstimate(flops=2 * 1024 * 5120 * 512, bytes_accessed=200 << 20, transcendentals=0),
    )(*operands)


def body(
    queries,
    leaf_keys,
    leaf_token_values,
    key_value_pages,
    page_holder,
    page_slot,
    segment_ids,
    req_parent,
    mid_parent,
    node_len,
    residual,
    out_proj,
    norm_gain,
    gate_proj,
    up_proj,
    down_proj,
    next_gain,
    qkv_proj,
    qkv_bias,
):
    return layer(
        queries,
        leaf_keys,
        leaf_token_values,
        key_value_pages.reshape(PAGES, PAGE, 2 * HEAD_SIZE),
        page_holder.transpose(1, 2, 0),
        page_slot.transpose(1, 2, 0),
        segment_ids.reshape(1, TOKENS),
        req_parent,
        mid_parent,
        node_len,
        residual,
        out_proj,
        norm_gain.reshape(1, -1),
        gate_proj.T,
        up_proj.T,
        down_proj,
        next_gain.reshape(1, -1),
        qkv_proj,
        qkv_bias.reshape(1, -1),
    )


def solution(mesh):
    placed = (
        P("req", "mlp"),
        P("req", "mlp"),
        P("req", "mlp"),
        P("req", None, None, "mlp"),
        P(),
        P(),
        P("req"),
        P("req", None),
        P("req", None),
        P("req", None),
        P("req", None),
        P("mlp", None),
        P(),
        P(None, ("req", "mlp")),
        P(None, ("req", "mlp")),
        P(("req", "mlp"), None),
        P(),
        P(None, "mlp"),
        P("mlp"),
    )
    return jax.shard_map(
        body,
        mesh=mesh,
        in_specs=placed,
        out_specs=(P(("req", "mlp"), None), P("req", "mlp")),
        check_vma=False,
    )
```

```python
import functools
import math

import jax
import jax.numpy as jnp
from jax import lax
from jax.experimental import pallas as pl
from jax.experimental.pallas import tpu as pltpu
from jax.sharding import PartitionSpec as P

HEAD_SIZE = 128
QUERY_PER_KV = 5
REQ_DEV = 8
ROOT_DEV = 2
MID_DEV = 4
NODES_DEV = 6
NODE_MAX = 256
MODEL = 5120
ROWS = 16
UNITS = 108
UNITS_PAD = 128
DOWN_PAD = 112
QKV_COLS = 896
TOKENS = 128
PAGES = 32
PAGE = 64
ENTRIES = 24
PREFIX = NODES_DEV * NODE_MAX
SLICES = 4
CHUNKS = 4
HIDDEN = -1e30

EPS = 1e-06

MESH = pl.DeviceIdType.MESH


def place():
    req = lax.axis_index("req")
    mlp = lax.axis_index("mlp")
    return lax.div(mlp, 2), lax.div(req, 4), lax.rem(req, 4), lax.rem(mlp, 2)


def device(x, y, z, core):
    return (y * 4 + z, x * 2 + core)


def ahead(coords, axis, steps):
    moved = list(coords)
    moved[axis] = lax.rem(moved[axis] + steps, 4)
    return moved


def greet(others):
    barrier = pltpu.get_barrier_semaphore()
    for other in others:
        pl.semaphore_signal(barrier, inc=1, device_id=other, device_id_type=MESH)


def greeted(others):
    pl.semaphore_wait(pltpu.get_barrier_semaphore(), len(others))


def lines_through(x, y, z, core):
    others = [device(x, y, z, 1 - core)]
    for axis in range(3):
        for steps in (1, 2, 3):
            others.append(device(*ahead((x, y, z), axis, steps), core))
    return others


def remote(src, dst, send, recv, target):
    return pltpu.make_async_remote_copy(
        src_ref=src, dst_ref=dst, send_sem=send, recv_sem=recv, device_id=target, device_id_type=MESH
    )


def normed_rows(rows, gain):
    mean_sq = jnp.mean(rows * rows, axis=-1, keepdims=True)
    return (rows * lax.rsqrt(mean_sq + EPS) * gain).astype(jnp.bfloat16)


PARTS = (
    (0, 1024, 512, (1, 2, 0)),
    (1024, 2048, 1024, (0, 1, 2)),
    (3072, 2048, 1024, (0, 2, 1)),
)


def layer_kernel(
    queries,
    leaf_keys,
    leaf_values,
    pages_hbm,
    holder,
    slot,
    segment_row,
    req_parent,
    mid_parent,
    node_len,
    residual,
    out_hbm,
    gain,
    gate_hbm,
    up_hbm,
    down_hbm,
    next_gain,
    qkv_hbm,
    bias,
    layer_out,
    qkv_out,
    pages,
    outgoing,
    incoming,
    keys,
    values,
    hide,
    attention,
    out_proj,
    gate_up,
    own_down,
    projected,
    resid,
    half,
    summed,
    arrived,
    tokens,
    weights,
    hidden,
    hidden_in,
    sums_f32,
    down,
    qkv,
    first_in,
    second,
    second_in,
    rows,
    local_sem,
    page_send,
    page_recv,
    half_send,
    half_recv,
    sum_send,
    sum_recv,
    weight_sem,
    part_send,
    part_recv,
    hid_send,
    hid_recv,
    down_send,
    down_recv,
    twin_send,
    twin_recv,
    first_send,
    first_recv,
    second_send,
    second_recv,
    row_send,
    row_recv,
):
    x, y, z, core = place()
    here = (x, y, z)
    group = lax.axis_index("req")
    sibling = device(x, y, z, 1 - core)
    own_rows = pl.multiple_of((x * 2 + core) * ROWS, ROWS)
    own_cols = pl.multiple_of(core * 2 * UNITS_PAD, 2 * UNITS_PAD)
    mine = x * 2 + core
    others = lines_through(x, y, z, core)
    plane = []
    for offset in range(1, 16):
        spot = (x, lax.rem(y + offset // 4, 4), lax.rem(z + offset % 4, 4))
        plane.append(spot)
        if offset // 4 and offset % 4:
            others.append(device(*spot, core))
    greet(others)

    def local(src, dst, index):
        copy = pltpu.make_async_copy(src, dst, local_sem.at[index])
        copy.start()
        return copy

    pages_copy = local(pages_hbm, pages, 0)
    gate_copy = local(gate_hbm, gate_up.at[0], 1)
    up_copy = local(up_hbm, gate_up.at[1], 2)
    down_copy = local(down_hbm, own_down, 5)
    out_copy = local(out_hbm, out_proj, 3)
    resid_copy = local(residual.at[pl.ds(own_rows, ROWS), :], resid, 4)
    qkv_copy = local(qkv_hbm, qkv, 6)

    pages_copy.wait()
    for number, spot in enumerate(plane):
        asker = spot[1] * 4 + spot[2]
        picked = jnp.int32(0)
        for entry in range(ENTRIES):
            picked = jnp.where(holder[entry // 4, entry % 4, asker] == group, slot[entry // 4, entry % 4, asker], picked)
        outgoing[number] = pages[picked]
    greeted(others)
    fetched = []
    for number in range(14, -1, -1):
        copy = remote(
            outgoing.at[number],
            incoming.at[group],
            page_send.at[number],
            page_recv.at[number],
            device(*plane[number], core),
        )
        copy.start()
        fetched.append(copy)

    gate_copy.wait()
    up_copy.wait()
    for which in range(2):
        cols = pl.ds(pl.multiple_of(own_cols + which * UNITS_PAD, UNITS_PAD), UNITS_PAD)
        weights[:, cols] = jnp.concatenate(
            [gate_up[which], jnp.zeros((UNITS_PAD - UNITS, MODEL), jnp.bfloat16)], axis=0
        ).T
    spot = weights.at[:, pl.ds(own_cols, 2 * UNITS_PAD)]
    swap = remote(spot, spot, weight_sem.at[0], weight_sem.at[1], sibling)
    swap.start()

    twins = []
    downs = []

    def down_block(offset, first, width):
        member = lax.rem(x + offset, 4) * 2 + core
        return down.at[member, pl.ds(0, DOWN_PAD), pl.ds(first, width)]

    def down_push(kind, part, way, offset, first, width):
        view = down_block(offset, first, width)
        copy = remote(
            view,
            view,
            down_send.at[kind, part, way],
            down_recv.at[kind, part, way],
            device(*ahead(here, 0, (1, 3)[way]), core),
        )
        copy.start()
        downs.append(copy)
        return copy

    def twin(offset):
        view = down_block(offset, 0, MODEL)
        copy = remote(view, view, twin_send.at[offset], twin_recv.at[offset], sibling)
        copy.start()
        twins.append(copy)

    wide = MODEL // 2

    def down_direct(part):
        return [down_push(0, part, way, 0, part * wide, wide) for way in range(2)]

    def down_onward(part):
        return [
            down_push(1, part, way, behind, part * wide + way * (wide // 2), wide // 2)
            for way, behind in enumerate((3, 1))
        ]

    down_copy.wait()
    down[mine, pl.ds(0, DOWN_PAD), :] = jnp.concatenate(
        [own_down[...], jnp.zeros((DOWN_PAD - UNITS, MODEL), jnp.bfloat16)], axis=0
    )
    for member in range(8):
        down[member, pl.ds(DOWN_PAD, UNITS_PAD - DOWN_PAD), :] = jnp.zeros(
            (UNITS_PAD - DOWN_PAD, MODEL), jnp.bfloat16
        )
    down_near = [down_direct(0)]

    line = segment_row[...]
    across = lax.broadcasted_iota(jnp.int32, (TOKENS, TOKENS), 1)
    along = lax.broadcasted_iota(jnp.int32, (TOKENS, TOKENS), 0)
    segments = jnp.sum(jnp.where(across == along, line, 0), axis=1, keepdims=True)
    middle = jnp.zeros_like(segments)
    for request in range(REQ_DEV):
        middle = jnp.where(segments == request, req_parent[0, request], middle)
    root = jnp.zeros_like(segments)
    for node in range(MID_DEV):
        root = jnp.where(middle == node, mid_parent[0, node], root)
    position = lax.broadcasted_iota(jnp.int32, (TOKENS, NODE_MAX), 1)
    for node in range(NODES_DEV):
        chosen = root == node if node < ROOT_DEV else middle == node - ROOT_DEV
        length = jnp.where(chosen, node_len[0, node], 0)
        hide[:, node * NODE_MAX : (node + 1) * NODE_MAX] = jnp.where(position < length, 0.0, HIDDEN)
    hide[:, PREFIX:] = jnp.where((segments == line) & (across <= along), 0.0, HIDDEN)

    for copy in fetched:
        copy.wait_recv()
    for entry in range(ENTRIES):
        kept = holder[entry // 4, entry % 4, group]
        page = jnp.where(kept == group, pages[slot[entry // 4, entry % 4, group]], incoming[kept])
        keys[entry * PAGE : (entry + 1) * PAGE, :] = page[:, :HEAD_SIZE]
        values[entry * PAGE : (entry + 1) * PAGE, :] = page[:, HEAD_SIZE:]
    keys[PREFIX:, :] = leaf_keys[...]
    values[PREFIX:, :] = leaf_values[...]
    for head in range(QUERY_PER_KV):
        cols = slice(head * HEAD_SIZE, (head + 1) * HEAD_SIZE)
        score = lax.dot_general(
            queries[:, cols], keys[...], (((1,), (1,)), ((), ())), preferred_element_type=jnp.float32
        )
        score = score * (1.0 / math.sqrt(HEAD_SIZE)) + hide[...]
        expo = jnp.exp(score - jnp.max(score, axis=1, keepdims=True))
        total = jnp.sum(expo, axis=1, keepdims=True)
        seen = jnp.dot(expo.astype(jnp.bfloat16), values[...], preferred_element_type=jnp.float32)
        attention[:, cols] = (seen / total).astype(jnp.bfloat16)

    out_copy.wait()
    size = MODEL // SLICES
    halves = []
    for piece in range(SLICES):
        cols = slice(piece * size, (piece + 1) * size)
        term = jnp.dot(attention[...], out_proj[:, cols], preferred_element_type=jnp.float32)
        term = term.astype(jnp.bfloat16).reshape(4, 2, ROWS, size)
        projected[0, :, :, cols] = term[:, 0]
        projected[1, :, :, cols] = term[:, 1]
        copy = remote(
            projected.at[1 - core, :, :, cols],
            half.at[:, :, cols],
            half_send.at[piece],
            half_recv.at[piece],
            sibling,
        )
        copy.start()
        halves.append(copy)
    sums = []
    for piece in range(SLICES):
        cols = slice(piece * size, (piece + 1) * size)
        halves[piece].wait_recv()
        for steps in (2, 1, 3):
            chip = lax.rem(x + steps, 4)
            summed[steps, :, cols] = (
                projected[core, chip, :, cols].astype(jnp.float32) + half[chip, :, cols].astype(jnp.float32)
            ).astype(jnp.bfloat16)
            copy = remote(
                summed.at[steps, :, cols],
                arrived.at[steps, :, cols],
                sum_send.at[piece, steps - 1],
                sum_recv.at[piece, steps - 1],
                device(*ahead(here, 0, steps), core),
            )
            copy.start()
            sums.append(copy)
    total = projected[core, x].astype(jnp.float32) + half[x].astype(jnp.float32)
    for copy in sums:
        copy.wait_recv()
    for steps in (1, 2, 3):
        total = total + arrived[steps].astype(jnp.float32)
    resid_copy.wait()
    stream = (resid[...].astype(jnp.float32) + total).astype(jnp.bfloat16)
    tokens[x, y, z] = normed_rows(stream.astype(jnp.float32), gain[...])

    def block(part, offsets, half=None):
        first, width, cut, order = PARTS[part]
        if half is not None:
            first, width = ((first, cut), (first + cut, width - cut))[half]
        index = [slice(None)] * 3
        for axis, offset in zip(order, offsets):
            if offset is not None:
                index[axis] = lax.rem(here[axis] + offset, 4)
        return (index[0], index[1], index[2], slice(None), pl.ds(first, width))

    pending = []

    def push(part, phase, slot, way, spot):
        view = tokens.at[spot]
        copy = remote(
            view,
            view,
            part_send.at[part, phase, slot, way],
            part_recv.at[part, phase, slot, way],
            device(*ahead(here, PARTS[part][3][phase], (1, 3)[way]), core),
        )
        copy.start()
        pending.append(copy)
        return copy

    def both_ways(part, phase, slot, offsets):
        spot = block(part, offsets)
        return [push(part, phase, slot, way, spot) for way in range(2)]

    def onward(part, phase, slot, offsets):
        return [
            push(part, phase, slot, way, block(part, offsets[:phase] + (behind,) + offsets[phase + 1 :], way))
            for way, behind in enumerate((3, 1))
        ]

    def arrive(copies):
        for copy in copies:
            copy.wait_recv()

    def product(part, offset):
        first, width, _, order = PARTS[part]
        index = [slice(None)] * 3
        index[order[2]] = lax.rem(here[order[2]] + offset, 4)
        rows = tokens[index[0], index[1], index[2], :, pl.ds(first, width)].reshape(256, width)
        term = jnp.dot(rows, weights[pl.ds(first, width), :], preferred_element_type=jnp.float32)
        spot = (index[0], index[1], index[2])
        shape = [4, 4, 4]
        del shape[order[2]]
        sums_f32[spot] += term.reshape(*shape, ROWS, 4 * UNITS_PAD)

    every = range(3)
    near = [both_ways(part, 0, 0, (0, 0, 0)) for part in every]
    lines = [both_ways(part, 1, 0, (0, 0, 0)) for part in every]
    twin(0)
    sums_f32[...] = jnp.zeros_like(sums_f32)
    far = []
    for part in every:
        arrive(near[part])
        far.append(onward(part, 0, 1, (0, 0, 0)))
        for slot, offset in ((1, 1), (2, 3)):
            lines[part] += both_ways(part, 1, slot, (offset, 0, 0))
    planes = [[None] * 4 for _ in every]
    for part in every:
        arrive(far[part])
        lines[part] += both_ways(part, 1, 3, (2, 0, 0))
        planes[part][0] = both_ways(part, 2, 0, (None, 0, 0))
    arrive(down_near[0])
    down_far = down_onward(0)
    down_near.append(down_direct(1))
    far = []
    for part in every:
        arrive(lines[part])
        far.append(onward(part, 1, 4, (None, 0, 0)))
        for offset in (1, 3):
            planes[part][offset] = both_ways(part, 2, offset, (None, offset, 0))
    for part in every:
        arrive(far[part])
        planes[part][2] = both_ways(part, 2, 2, (None, 2, 0))
    swap.wait_recv()
    last = []
    for offset in (0, 1, 3, 2):
        for part in every:
            arrive(planes[part][offset])
            last += onward(part, 2, 4 + offset, (None, offset, 0))
        if offset in (0, 1, 3):
            product((0, 1, None, 2)[offset], 0)
        if offset == 1:
            arrive(down_near[1])
            down_far += down_onward(1)
            twin(1)
            twin(3)
    for part in every:
        product(part, 1)
        product(part, 3)
    arrive(down_far)
    twin(2)
    arrive(last)
    for part in every:
        product(part, 2)

    given = []
    spot = hidden_in.at[:, pl.ds(pl.multiple_of(x * 2 * UNITS_PAD, 2 * UNITS_PAD), 2 * UNITS_PAD)]
    for steps in (2, 1, 3, 0):
        target = ahead(here, 0, steps)
        chip = target[0]
        both = sums_f32[chip].reshape(256, 4 * UNITS_PAD)
        outs = []
        for which in range(2):
            gate = both[:, which * 2 * UNITS_PAD : which * 2 * UNITS_PAD + UNITS_PAD]
            upper = both[:, which * 2 * UNITS_PAD + UNITS_PAD : (which + 1) * 2 * UNITS_PAD]
            outs.append((gate / (1.0 + jnp.exp(-gate)) * upper).astype(jnp.bfloat16))
        if steps:
            hidden[steps - 1] = jnp.concatenate(outs, axis=1)
            copy = remote(
                hidden.at[steps - 1], spot, hid_send.at[steps - 1], hid_recv.at[steps - 1], device(*target, core)
            )
            copy.start()
            given.append(copy)
        else:
            spot[...] = jnp.concatenate(outs, axis=1)
    for copy in pending:
        copy.wait_send()
    partial = tokens.at[0]
    arrive(given)
    arrive(twins)

    size = MODEL // CHUNKS
    sent = []
    firsts = []
    for chunk in range(CHUNKS):
        cols = pl.ds(chunk * size, size)
        total = jnp.dot(
            hidden_in[...],
            down[:, :, chunk * size : (chunk + 1) * size].reshape(8 * UNITS_PAD, size),
            preferred_element_type=jnp.float32,
        )
        partial[:, :, :, cols] = total.astype(jnp.bfloat16).reshape(4, 4, ROWS, size)
        axis = 1 + chunk % 2
        copies = []
        for steps in (2, 1, 3):
            target = ahead(here, axis, steps)
            src = partial.at[target[1], :, :, cols] if axis == 1 else partial.at[:, target[2], :, cols]
            copy = remote(
                src,
                first_in.at[chunk, steps - 1],
                first_send.at[chunk, steps - 1],
                first_recv.at[chunk, steps - 1],
                device(*target, core),
            )
            copy.start()
            copies.append(copy)
        firsts.append(copies)
        sent += copies
    seconds = []
    for chunk in range(CHUNKS):
        cols = pl.ds(chunk * size, size)
        axis = 1 + chunk % 2
        for copy in firsts[chunk]:
            copy.wait_recv()
        own = partial[y, :, :, cols] if axis == 1 else partial[:, z, :, cols]
        total = own.astype(jnp.float32)
        for steps in range(3):
            total = total + first_in[chunk, steps].astype(jnp.float32)
        second[chunk] = total.astype(jnp.bfloat16)
        copies = []
        for steps in (2, 1, 3):
            target = ahead(here, 3 - axis, steps)
            copy = remote(
                second.at[chunk, target[3 - axis]],
                second_in.at[chunk, steps - 1],
                second_send.at[chunk, steps - 1],
                second_recv.at[chunk, steps - 1],
                device(*target, core),
            )
            copy.start()
            copies.append(copy)
        seconds.append(copies)
        sent += copies
    parts = []
    for chunk in range(CHUNKS):
        axis = 1 + chunk % 2
        for copy in seconds[chunk]:
            copy.wait_recv()
        total = second[chunk, here[3 - axis]].astype(jnp.float32)
        for steps in range(3):
            total = total + second_in[chunk, steps].astype(jnp.float32)
        parts.append(total)
    mixed = jnp.concatenate(parts, axis=1)
    out = (stream.astype(jnp.float32) + mixed).astype(jnp.bfloat16)
    layer_out[...] = out
    rows[mine] = normed_rows(out.astype(jnp.float32), next_gain[...])
    ring = []
    for steps in (2, 1, 3):
        copy = remote(
            rows.at[mine],
            rows.at[mine],
            row_send.at[steps - 1],
            row_recv.at[steps - 1],
            device(*ahead(here, 0, steps), core),
        )
        copy.start()
        ring.append((steps, copy))
    passed = []
    copy = remote(rows.at[mine], rows.at[mine], row_send.at[3], row_recv.at[3], sibling)
    copy.start()
    passed.append(copy)
    for steps, arrival in reversed(ring):
        arrival.wait_recv()
        other = lax.rem(x + 4 - steps, 4) * 2 + core
        copy = remote(rows.at[other], rows.at[other], row_send.at[3 + steps], row_recv.at[3 + steps], sibling)
        copy.start()
        passed.append(copy)
    for copy in passed:
        copy.wait_recv()
    qkv_copy.wait()
    result = jnp.dot(rows[...].reshape(8 * ROWS, MODEL), qkv[...], preferred_element_type=jnp.float32)
    qkv_out[...] = (result + bias[...]).astype(jnp.bfloat16)
    for copy in fetched + halves + sums + [swap] + downs + twins + given + sent + [copy for _, copy in ring] + passed:
        copy.wait_send()


def layer(*operands):
    vmem = pl.BlockSpec(memory_space=pltpu.VMEM)
    smem = pl.BlockSpec(memory_space=pltpu.SMEM)
    anywhere = pl.BlockSpec(memory_space=pl.ANY)
    dma = pltpu.SemaphoreType.DMA

    def held(*shape):
        return pltpu.VMEM(shape, jnp.bfloat16)

    size = MODEL // CHUNKS
    return pl.pallas_call(
        layer_kernel,
        out_shape=(
            jax.ShapeDtypeStruct((ROWS, MODEL), jnp.bfloat16),
            jax.ShapeDtypeStruct((TOKENS, QKV_COLS), jnp.bfloat16),
        ),
        in_specs=[vmem] * 3
        + [anywhere, smem, smem, vmem, smem, smem, smem, anywhere, anywhere, vmem]
        + [anywhere, anywhere, anywhere, vmem, anywhere, vmem],
        out_specs=(vmem, vmem),
        scratch_shapes=[
            held(PAGES, PAGE, 2 * HEAD_SIZE),
            held(15, PAGE, 2 * HEAD_SIZE),
            held(16, PAGE, 2 * HEAD_SIZE),
            held(PREFIX + TOKENS, HEAD_SIZE),
            held(PREFIX + TOKENS, HEAD_SIZE),
            pltpu.VMEM((TOKENS, PREFIX + TOKENS), jnp.float32),
            held(TOKENS, QUERY_PER_KV * HEAD_SIZE),
            held(QUERY_PER_KV * HEAD_SIZE, MODEL),
            held(2, UNITS, MODEL),
            held(UNITS, MODEL),
            held(2, 4, ROWS, MODEL),
            held(ROWS, MODEL),
            held(4, ROWS, MODEL),
            held(4, ROWS, MODEL),
            held(4, ROWS, MODEL),
            held(4, 4, 4, ROWS, MODEL),
            held(MODEL, 4 * UNITS_PAD),
            held(3, 256, 2 * UNITS_PAD),
            held(256, 8 * UNITS_PAD),
            pltpu.VMEM((4, 4, 4, ROWS, 4 * UNITS_PAD), jnp.float32),
            held(8, UNITS_PAD, MODEL),
            held(MODEL, QKV_COLS),
            held(CHUNKS, 3, 4, ROWS, size),
            held(CHUNKS, 4, ROWS, size),
            held(CHUNKS, 3, ROWS, size),
            held(8, ROWS, MODEL),
            dma((7,)),
            dma((15,)),
            dma((15,)),
            dma((SLICES,)),
            dma((SLICES,)),
            dma((SLICES, 3)),
            dma((SLICES, 3)),
            dma((2,)),
            dma((3, 3, 8, 2)),
            dma((3, 3, 8, 2)),
            dma((3,)),
            dma((3,)),
            dma((2, 2, 2)),
            dma((2, 2, 2)),
            dma((4,)),
            dma((4,)),
            dma((CHUNKS, 3)),
            dma((CHUNKS, 3)),
            dma((CHUNKS, 3)),
            dma((CHUNKS, 3)),
            dma((7,)),
            dma((7,)),
        ],
        compiler_params=pltpu.CompilerParams(
            collective_id=0, has_side_effects=True, vmem_limit_bytes=63 << 20
        ),
        cost_estimate=pl.CostEstimate(flops=2 * 1024 * 5120 * 512, bytes_accessed=200 << 20, transcendentals=0),
    )(*operands)


def body(
    queries,
    leaf_keys,
    leaf_token_values,
    key_value_pages,
    page_holder,
    page_slot,
    segment_ids,
    req_parent,
    mid_parent,
    node_len,
    residual,
    out_proj,
    norm_gain,
    gate_proj,
    up_proj,
    down_proj,
    next_gain,
    qkv_proj,
    qkv_bias,
):
    return layer(
        queries,
        leaf_keys,
        leaf_token_values,
        key_value_pages.reshape(PAGES, PAGE, 2 * HEAD_SIZE),
        page_holder.transpose(1, 2, 0),
        page_slot.transpose(1, 2, 0),
        segment_ids.reshape(1, TOKENS),
        req_parent,
        mid_parent,
        node_len,
        residual,
        out_proj,
        norm_gain.reshape(1, -1),
        gate_proj.T,
        up_proj.T,
        down_proj,
        next_gain.reshape(1, -1),
        qkv_proj,
        qkv_bias.reshape(1, -1),
    )


def solution(mesh):
    placed = (
        P("req", "mlp"),
        P("req", "mlp"),
        P("req", "mlp"),
        P("req", None, None, "mlp"),
        P(),
        P(),
        P("req"),
        P("req", None),
        P("req", None),
        P("req", None),
        P("req", None),
        P("mlp", None),
        P(),
        P(None, ("req", "mlp")),
        P(None, ("req", "mlp")),
        P(("req", "mlp"), None),
        P(),
        P(None, "mlp"),
        P("mlp"),
    )
    return jax.shard_map(
        body,
        mesh=mesh,
        in_specs=placed,
        out_specs=(P(("req", "mlp"), None), P("req", "mlp")),
        check_vma=False,
    )
```

```python
import functools
import math

import jax
import jax.numpy as jnp
from jax import lax
from jax.experimental import pallas as pl
from jax.experimental.pallas import tpu as pltpu
from jax.sharding import PartitionSpec as P

HEAD_SIZE = 128
QUERY_PER_KV = 5
REQ_DEV = 8
ROOT_DEV = 2
MID_DEV = 4
NODES_DEV = 6
NODE_MAX = 256
MODEL = 5120
ROWS = 16
UNITS = 108
UNITS_PAD = 128
DOWN_PAD = 112
QKV_COLS = 896
TOKENS = 128
PAGES = 32
PAGE = 64
ENTRIES = 24
PREFIX = NODES_DEV * NODE_MAX
SLICES = 5
CHUNKS = 4
HIDDEN = -1e30

EPS = 1e-06

MESH = pl.DeviceIdType.MESH


def place():
    req = lax.axis_index("req")
    mlp = lax.axis_index("mlp")
    return lax.div(mlp, 2), lax.div(req, 4), lax.rem(req, 4), lax.rem(mlp, 2)


def device(x, y, z, core):
    return (y * 4 + z, x * 2 + core)


def ahead(coords, axis, steps):
    moved = list(coords)
    moved[axis] = lax.rem(moved[axis] + steps, 4)
    return moved


def greet(others):
    barrier = pltpu.get_barrier_semaphore()
    for other in others:
        pl.semaphore_signal(barrier, inc=1, device_id=other, device_id_type=MESH)


def greeted(others):
    pl.semaphore_wait(pltpu.get_barrier_semaphore(), len(others))


def lines_through(x, y, z, core):
    others = [device(x, y, z, 1 - core)]
    for axis in range(3):
        for steps in (1, 2, 3):
            others.append(device(*ahead((x, y, z), axis, steps), core))
    return others


def remote(src, dst, send, recv, target):
    return pltpu.make_async_remote_copy(
        src_ref=src, dst_ref=dst, send_sem=send, recv_sem=recv, device_id=target, device_id_type=MESH
    )


def normed_rows(rows, gain):
    mean_sq = jnp.mean(rows * rows, axis=-1, keepdims=True)
    return (rows * lax.rsqrt(mean_sq + EPS) * gain).astype(jnp.bfloat16)


PARTS = (
    (0, 1024, 512, (1, 2, 0)),
    (1024, 2048, 1024, (0, 1, 2)),
    (3072, 2048, 1024, (0, 2, 1)),
)


def layer_kernel(
    queries,
    leaf_keys,
    leaf_values,
    pages_hbm,
    holder,
    slot,
    segment_row,
    req_parent,
    mid_parent,
    node_len,
    residual,
    out_hbm,
    gain,
    gate_hbm,
    up_hbm,
    down_hbm,
    next_gain,
    qkv_hbm,
    bias,
    layer_out,
    qkv_out,
    pages,
    outgoing,
    incoming,
    keys,
    values,
    hide,
    attention,
    out_proj,
    gate_up,
    own_down,
    projected,
    resid,
    half,
    summed,
    arrived,
    tokens,
    wide_weights,
    hidden,
    hidden_in,
    sums_f32,
    squares,
    down,
    first_in,
    second,
    second_in,
    rows,
    local_sem,
    page_send,
    page_recv,
    half_send,
    half_recv,
    sum_send,
    sum_recv,
    weight_sem,
    part_send,
    part_recv,
    hid_send,
    hid_recv,
    down_send,
    down_recv,
    twin_send,
    twin_recv,
    first_send,
    first_recv,
    second_send,
    second_recv,
    row_send,
    row_recv,
):
    x, y, z, core = place()
    here = (x, y, z)
    group = lax.axis_index("req")
    sibling = device(x, y, z, 1 - core)
    own_rows = pl.multiple_of((x * 2 + core) * ROWS, ROWS)
    own_cols = pl.multiple_of(core * 2 * UNITS_PAD, 2 * UNITS_PAD)
    mine = x * 2 + core
    weights = wide_weights.at[:, 0 : 4 * UNITS_PAD]
    others = lines_through(x, y, z, core)
    plane = []
    for offset in range(1, 16):
        spot = (x, lax.rem(y + offset // 4, 4), lax.rem(z + offset % 4, 4))
        plane.append(spot)
        if offset // 4 and offset % 4:
            others.append(device(*spot, core))
    greet(others)

    def local(src, dst, index):
        copy = pltpu.make_async_copy(src, dst, local_sem.at[index])
        copy.start()
        return copy

    pages_copy = local(pages_hbm, pages, 0)
    down_copy = local(down_hbm, own_down, 5)
    gate_copy = local(gate_hbm, gate_up.at[0], 1)
    up_copy = local(up_hbm, gate_up.at[1], 2)
    out_copy = local(out_hbm, out_proj, 3)
    resid_copy = local(residual.at[pl.ds(own_rows, ROWS), :], resid, 4)

    pages_copy.wait()
    for number, spot in enumerate(plane):
        asker = spot[1] * 4 + spot[2]
        picked = jnp.int32(0)
        for entry in range(ENTRIES):
            picked = jnp.where(holder[entry // 4, entry % 4, asker] == group, slot[entry // 4, entry % 4, asker], picked)
        outgoing[number] = pages[picked]
    greeted(others)
    fetched = []
    for number in range(14, -1, -1):
        copy = remote(
            outgoing.at[number],
            incoming.at[group],
            page_send.at[number],
            page_recv.at[number],
            device(*plane[number], core),
        )
        copy.start()
        fetched.append(copy)

    twins = []
    downs = []

    def down_block(offset, first, width):
        member = lax.rem(x + offset, 4) * 2 + core
        return down.at[member, pl.ds(0, DOWN_PAD), pl.ds(first, width)]

    def down_push(kind, part, way, offset, first, width):
        view = down_block(offset, first, width)
        copy = remote(
            view,
            view,
            down_send.at[kind, part, way],
            down_recv.at[kind, part, way],
            device(*ahead(here, 0, (1, 3)[way]), core),
        )
        copy.start()
        downs.append(copy)
        return copy

    def twin(offset):
        view = down_block(offset, 0, MODEL)
        copy = remote(view, view, twin_send.at[offset], twin_recv.at[offset], sibling)
        copy.start()
        twins.append(copy)

    wide = MODEL // 2

    def down_direct(part):
        return [down_push(0, part, way, 0, part * wide, wide) for way in range(2)]

    def down_onward(part):
        return [
            down_push(1, part, way, behind, part * wide + way * (wide // 2), wide // 2)
            for way, behind in enumerate((3, 1))
        ]

    down_copy.wait()
    down[mine, pl.ds(0, DOWN_PAD), :] = jnp.concatenate(
        [own_down[...], jnp.zeros((DOWN_PAD - UNITS, MODEL), jnp.bfloat16)], axis=0
    )
    for member in range(8):
        down[member, pl.ds(DOWN_PAD, UNITS_PAD - DOWN_PAD), :] = jnp.zeros(
            (UNITS_PAD - DOWN_PAD, MODEL), jnp.bfloat16
        )
    down_near = [down_direct(0)]

    line = segment_row[...]
    across = lax.broadcasted_iota(jnp.int32, (TOKENS, TOKENS), 1)
    along = lax.broadcasted_iota(jnp.int32, (TOKENS, TOKENS), 0)
    segments = jnp.sum(jnp.where(across == along, line, 0), axis=1, keepdims=True)
    middle = jnp.zeros_like(segments)
    for request in range(REQ_DEV):
        middle = jnp.where(segments == request, req_parent[0, request], middle)
    root = jnp.zeros_like(segments)
    for node in range(MID_DEV):
        root = jnp.where(middle == node, mid_parent[0, node], root)
    position = lax.broadcasted_iota(jnp.int32, (TOKENS, NODE_MAX), 1)
    for node in range(NODES_DEV):
        chosen = root == node if node < ROOT_DEV else middle == node - ROOT_DEV
        length = jnp.where(chosen, node_len[0, node], 0)
        hide[:, node * NODE_MAX : (node + 1) * NODE_MAX] = jnp.where(position < length, 0.0, HIDDEN)
    hide[:, PREFIX:] = jnp.where((segments == line) & (across <= along), 0.0, HIDDEN)

    for copy in fetched:
        copy.wait_recv()
    for entry in range(ENTRIES):
        kept = holder[entry // 4, entry % 4, group]
        page = jnp.where(kept == group, pages[slot[entry // 4, entry % 4, group]], incoming[kept])
        keys[entry * PAGE : (entry + 1) * PAGE, :] = page[:, :HEAD_SIZE]
        values[entry * PAGE : (entry + 1) * PAGE, :] = page[:, HEAD_SIZE:]
    keys[PREFIX:, :] = leaf_keys[...]
    values[PREFIX:, :] = leaf_values[...]
    for head in range(QUERY_PER_KV):
        cols = slice(head * HEAD_SIZE, (head + 1) * HEAD_SIZE)
        score = lax.dot_general(
            queries[:, cols], keys[...], (((1,), (1,)), ((), ())), preferred_element_type=jnp.float32
        )
        score = score * (1.0 / math.sqrt(HEAD_SIZE)) + hide[...]
        expo = jnp.exp(score - jnp.max(score, axis=1, keepdims=True))
        total = jnp.sum(expo, axis=1, keepdims=True)
        seen = jnp.dot(expo.astype(jnp.bfloat16), values[...], preferred_element_type=jnp.float32)
        attention[:, cols] = (seen / total).astype(jnp.bfloat16)

    out_copy.wait()
    size = MODEL // SLICES
    halves = []
    for piece in range(SLICES):
        cols = slice(piece * size, (piece + 1) * size)
        term = jnp.dot(attention[...], out_proj[:, cols], preferred_element_type=jnp.float32)
        term = term.astype(jnp.bfloat16).reshape(4, 2, ROWS, size)
        projected[0, :, :, cols] = term[:, 0]
        projected[1, :, :, cols] = term[:, 1]
        copy = remote(
            projected.at[1 - core, :, :, cols],
            half.at[:, :, cols],
            half_send.at[piece],
            half_recv.at[piece],
            sibling,
        )
        copy.start()
        halves.append(copy)
    sums = []
    for piece in range(SLICES):
        cols = slice(piece * size, (piece + 1) * size)
        halves[piece].wait_recv()
        passing = []
        for steps in (2, 1, 3):
            chip = lax.rem(x + steps, 4)
            summed[steps, :, cols] = (
                projected[core, chip, :, cols].astype(jnp.float32) + half[chip, :, cols].astype(jnp.float32)
            ).astype(jnp.bfloat16)
            copy = remote(
                summed.at[steps, :, cols],
                arrived.at[steps, :, cols],
                sum_send.at[piece, steps - 1],
                sum_recv.at[piece, steps - 1],
                device(*ahead(here, 0, steps), core),
            )
            copy.start()
            passing.append(copy)
        sums.append(passing)
    gate_copy.wait()
    up_copy.wait()
    for which in range(2):
        cols = pl.ds(pl.multiple_of(own_cols + which * UNITS_PAD, UNITS_PAD), UNITS_PAD)
        weights[:, cols] = jnp.concatenate(
            [
                (gate_up[which].astype(jnp.float32) * gain[...]).astype(jnp.bfloat16),
                jnp.zeros((UNITS_PAD - UNITS, MODEL), jnp.bfloat16),
            ],
            axis=0,
        ).T
    spot = weights.at[:, pl.ds(own_cols, 2 * UNITS_PAD)]
    swap = remote(spot, spot, weight_sem.at[0], weight_sem.at[1], sibling)
    swap.start()

    def block(part, offsets, half=None):
        first, width, cut, order = PARTS[part]
        if half is not None:
            first, width = ((first, cut), (first + cut, width - cut))[half]
        index = [slice(None)] * 3
        for axis, offset in zip(order, offsets):
            if offset is not None:
                index[axis] = lax.rem(here[axis] + offset, 4)
        return (index[0], index[1], index[2], slice(None), pl.ds(first, width))

    pending = []

    def push(part, phase, slot, way, spot):
        view = tokens.at[spot]
        copy = remote(
            view,
            view,
            part_send.at[part, phase, slot, way],
            part_recv.at[part, phase, slot, way],
            device(*ahead(here, PARTS[part][3][phase], (1, 3)[way]), core),
        )
        copy.start()
        pending.append(copy)
        return copy

    def both_ways(part, phase, slot, offsets):
        spot = block(part, offsets)
        return [push(part, phase, slot, way, spot) for way in range(2)]

    def onward(part, phase, slot, offsets):
        return [
            push(part, phase, slot, way, block(part, offsets[:phase] + (behind,) + offsets[phase + 1 :], way))
            for way, behind in enumerate((3, 1))
        ]

    def arrive(copies):
        for copy in copies:
            copy.wait_recv()

    def product(part, offset):
        first, width, _, order = PARTS[part]
        index = [slice(None)] * 3
        index[order[2]] = lax.rem(here[order[2]] + offset, 4)
        rows = tokens[index[0], index[1], index[2], :, pl.ds(first, width)].reshape(256, width)
        exact = rows.astype(jnp.float32)
        square = jnp.broadcast_to(jnp.sum(exact * exact, axis=1, keepdims=True), (256, HEAD_SIZE))
        term = jnp.dot(rows, wide_weights[pl.ds(first, width), 0 : 4 * UNITS_PAD], preferred_element_type=jnp.float32)
        spot = (index[0], index[1], index[2])
        shape = [4, 4, 4]
        del shape[order[2]]
        sums_f32[spot] += term.reshape(*shape, ROWS, 4 * UNITS_PAD)
        squares[spot] += square.reshape(*shape, ROWS, HEAD_SIZE)

    every = range(3)
    near, lines = [], []
    resid_copy.wait()
    for piece in range(SLICES):
        cols = slice(piece * size, (piece + 1) * size)
        arrive(sums[piece])
        total = projected[core, x, :, cols].astype(jnp.float32) + half[x, :, cols].astype(jnp.float32)
        for steps in (1, 2, 3):
            total = total + arrived[steps, :, cols].astype(jnp.float32)
        stream = (resid[:, cols].astype(jnp.float32) + total).astype(jnp.bfloat16)
        resid[:, cols] = stream
        tokens[x, y, z, :, cols] = stream
        if piece % 2 == 0:
            near.append(both_ways(piece // 2, 0, 0, (0, 0, 0)))
            lines.append(both_ways(piece // 2, 1, 0, (0, 0, 0)))
    sums_f32[...] = jnp.zeros_like(sums_f32)
    squares[...] = jnp.zeros_like(squares)
    far = []
    for part in every:
        arrive(near[part])
        far.append(onward(part, 0, 1, (0, 0, 0)))
        for slot, offset in ((1, 1), (2, 3)):
            lines[part] += both_ways(part, 1, slot, (offset, 0, 0))
    planes = [[None] * 4 for _ in every]
    for part in every:
        arrive(far[part])
        lines[part] += both_ways(part, 1, 3, (2, 0, 0))
        planes[part][0] = both_ways(part, 2, 0, (None, 0, 0))
    arrive(down_near[0])
    down_far = down_onward(0)
    down_near.append(down_direct(1))
    twin(0)
    far = []
    for part in every:
        arrive(lines[part])
        far.append(onward(part, 1, 4, (None, 0, 0)))
        for offset in (1, 3):
            planes[part][offset] = both_ways(part, 2, offset, (None, offset, 0))
    for part in every:
        arrive(far[part])
        planes[part][2] = both_ways(part, 2, 2, (None, 2, 0))
    swap.wait_recv()
    last = []
    for offset in (0, 1, 3, 2):
        for part in every:
            arrive(planes[part][offset])
            last += onward(part, 2, 4 + offset, (None, offset, 0))
        if offset in (0, 1, 3):
            product((0, 1, None, 2)[offset], 0)
        if offset == 1:
            arrive(down_near[1])
            down_far += down_onward(1)
            twin(1)
            twin(3)
    for part in every:
        product(part, 1)
        product(part, 3)
    arrive(down_far)
    twin(2)
    arrive(last)
    for part in every:
        product(part, 2)

    swap.wait_send()
    qkv_copy = local(qkv_hbm, wide_weights, 6)
    given = []
    spot = hidden_in.at[:, pl.ds(pl.multiple_of(x * 2 * UNITS_PAD, 2 * UNITS_PAD), 2 * UNITS_PAD)]
    for steps in (2, 1, 3, 0):
        target = ahead(here, 0, steps)
        chip = target[0]
        factor = lax.rsqrt(squares[chip].reshape(256, HEAD_SIZE)[:, :1] * (1.0 / MODEL) + EPS)
        both = sums_f32[chip].reshape(256, 4 * UNITS_PAD) * factor
        outs = []
        for which in range(2):
            gate = both[:, which * 2 * UNITS_PAD : which * 2 * UNITS_PAD + UNITS_PAD]
            upper = both[:, which * 2 * UNITS_PAD + UNITS_PAD : (which + 1) * 2 * UNITS_PAD]
            outs.append((gate / (1.0 + jnp.exp(-gate)) * upper).astype(jnp.bfloat16))
        if steps:
            hidden[steps - 1] = jnp.concatenate(outs, axis=1)
            copy = remote(
                hidden.at[steps - 1], spot, hid_send.at[steps - 1], hid_recv.at[steps - 1], device(*target, core)
            )
            copy.start()
            given.append(copy)
        else:
            spot[...] = jnp.concatenate(outs, axis=1)
    for copy in pending:
        copy.wait_send()
    partial = tokens.at[0]
    arrive(given)
    arrive(twins)

    size = MODEL // CHUNKS
    sent = []
    firsts = []
    for chunk in range(CHUNKS):
        cols = pl.ds(chunk * size, size)
        total = jnp.dot(
            hidden_in[...],
            down[:, :, chunk * size : (chunk + 1) * size].reshape(8 * UNITS_PAD, size),
            preferred_element_type=jnp.float32,
        )
        partial[:, :, :, cols] = total.astype(jnp.bfloat16).reshape(4, 4, ROWS, size)
        axis = 1 + chunk % 2
        copies = []
        for steps in (2, 1, 3):
            target = ahead(here, axis, steps)
            src = partial.at[target[1], :, :, cols] if axis == 1 else partial.at[:, target[2], :, cols]
            copy = remote(
                src,
                first_in.at[chunk, steps - 1],
                first_send.at[chunk, steps - 1],
                first_recv.at[chunk, steps - 1],
                device(*target, core),
            )
            copy.start()
            copies.append(copy)
        firsts.append(copies)
        sent += copies
    seconds = []
    for chunk in range(CHUNKS):
        cols = pl.ds(chunk * size, size)
        axis = 1 + chunk % 2
        for copy in firsts[chunk]:
            copy.wait_recv()
        own = partial[y, :, :, cols] if axis == 1 else partial[:, z, :, cols]
        total = own.astype(jnp.float32)
        for steps in range(3):
            total = total + first_in[chunk, steps].astype(jnp.float32)
        second[chunk] = total.astype(jnp.bfloat16)
        copies = []
        for steps in (2, 1, 3):
            target = ahead(here, 3 - axis, steps)
            copy = remote(
                second.at[chunk, target[3 - axis]],
                second_in.at[chunk, steps - 1],
                second_send.at[chunk, steps - 1],
                second_recv.at[chunk, steps - 1],
                device(*target, core),
            )
            copy.start()
            copies.append(copy)
        seconds.append(copies)
        sent += copies
    parts = []
    for chunk in range(CHUNKS):
        axis = 1 + chunk % 2
        for copy in seconds[chunk]:
            copy.wait_recv()
        total = second[chunk, here[3 - axis]].astype(jnp.float32)
        for steps in range(3):
            total = total + second_in[chunk, steps].astype(jnp.float32)
        parts.append(total)
    mixed = jnp.concatenate(parts, axis=1)
    out = (resid[...].astype(jnp.float32) + mixed).astype(jnp.bfloat16)
    layer_out[...] = out
    rows[mine] = normed_rows(out.astype(jnp.float32), next_gain[...])
    ring = []
    passed = []

    def hand(slot, member, part, target):
        view = rows.at[member, :, pl.ds(part * wide, wide)]
        copy = remote(view, view, row_send.at[part, slot], row_recv.at[part, slot], target)
        copy.start()
        return copy

    for part in range(2):
        ring.append([(steps, hand(steps - 1, mine, part, device(*ahead(here, 0, steps), core))) for steps in (2, 1, 3)])
        passed.append([hand(3, mine, part, sibling)])
    for part in range(2):
        for steps, arrival in reversed(ring[part]):
            arrival.wait_recv()
            other = lax.rem(x + 4 - steps, 4) * 2 + core
            passed[part].append(hand(3 + steps, other, part, sibling))
    qkv_copy.wait()
    result = bias[...].reshape(1, QKV_COLS)
    for part in range(2):
        arrive(passed[part])
        result = result + jnp.dot(
            rows[:, :, part * wide : (part + 1) * wide].reshape(TOKENS, wide),
            wide_weights[part * wide : (part + 1) * wide, :],
            preferred_element_type=jnp.float32,
        )
    qkv_out[...] = result.astype(jnp.bfloat16)
    for copy in fetched + halves + sum(sums, []) + downs + twins + given + sent + [copy for pair in ring for _, copy in pair] + sum(passed, []):
        copy.wait_send()


def layer(*operands):
    vmem = pl.BlockSpec(memory_space=pltpu.VMEM)
    smem = pl.BlockSpec(memory_space=pltpu.SMEM)
    anywhere = pl.BlockSpec(memory_space=pl.ANY)
    dma = pltpu.SemaphoreType.DMA

    def held(*shape):
        return pltpu.VMEM(shape, jnp.bfloat16)

    size = MODEL // CHUNKS
    return pl.pallas_call(
        layer_kernel,
        out_shape=(
            jax.ShapeDtypeStruct((ROWS, MODEL), jnp.bfloat16),
            jax.ShapeDtypeStruct((TOKENS, QKV_COLS), jnp.bfloat16),
        ),
        in_specs=[vmem] * 3
        + [anywhere, smem, smem, vmem, smem, smem, smem, anywhere, anywhere, vmem]
        + [anywhere, anywhere, anywhere, vmem, anywhere, vmem],
        out_specs=(vmem, vmem),
        scratch_shapes=[
            held(PAGES, PAGE, 2 * HEAD_SIZE),
            held(15, PAGE, 2 * HEAD_SIZE),
            held(16, PAGE, 2 * HEAD_SIZE),
            held(PREFIX + TOKENS, HEAD_SIZE),
            held(PREFIX + TOKENS, HEAD_SIZE),
            pltpu.VMEM((TOKENS, PREFIX + TOKENS), jnp.float32),
            held(TOKENS, QUERY_PER_KV * HEAD_SIZE),
            held(QUERY_PER_KV * HEAD_SIZE, MODEL),
            held(2, UNITS, MODEL),
            held(UNITS, MODEL),
            held(2, 4, ROWS, MODEL),
            held(ROWS, MODEL),
            held(4, ROWS, MODEL),
            held(4, ROWS, MODEL),
            held(4, ROWS, MODEL),
            held(4, 4, 4, ROWS, MODEL),
            held(MODEL, QKV_COLS),
            held(3, 256, 2 * UNITS_PAD),
            held(256, 8 * UNITS_PAD),
            pltpu.VMEM((4, 4, 4, ROWS, 4 * UNITS_PAD), jnp.float32),
            pltpu.VMEM((4, 4, 4, ROWS, HEAD_SIZE), jnp.float32),
            held(8, UNITS_PAD, MODEL),
            held(CHUNKS, 3, 4, ROWS, size),
            held(CHUNKS, 4, ROWS, size),
            held(CHUNKS, 3, ROWS, size),
            held(8, ROWS, MODEL),
            dma((7,)),
            dma((15,)),
            dma((15,)),
            dma((SLICES,)),
            dma((SLICES,)),
            dma((SLICES, 3)),
            dma((SLICES, 3)),
            dma((2,)),
            dma((3, 3, 8, 2)),
            dma((3, 3, 8, 2)),
            dma((3,)),
            dma((3,)),
            dma((2, 2, 2)),
            dma((2, 2, 2)),
            dma((4,)),
            dma((4,)),
            dma((CHUNKS, 3)),
            dma((CHUNKS, 3)),
            dma((CHUNKS, 3)),
            dma((CHUNKS, 3)),
            dma((2, 7)),
            dma((2, 7)),
        ],
        compiler_params=pltpu.CompilerParams(
            collective_id=0, has_side_effects=True, vmem_limit_bytes=57 << 20
        ),
        cost_estimate=pl.CostEstimate(flops=2 * 1024 * 5120 * 512, bytes_accessed=200 << 20, transcendentals=0),
    )(*operands)


def body(
    queries,
    leaf_keys,
    leaf_token_values,
    key_value_pages,
    page_holder,
    page_slot,
    segment_ids,
    req_parent,
    mid_parent,
    node_len,
    residual,
    out_proj,
    norm_gain,
    gate_proj,
    up_proj,
    down_proj,
    next_gain,
    qkv_proj,
    qkv_bias,
):
    return layer(
        queries,
        leaf_keys,
        leaf_token_values,
        key_value_pages.reshape(PAGES, PAGE, 2 * HEAD_SIZE),
        page_holder.transpose(1, 2, 0),
        page_slot.transpose(1, 2, 0),
        segment_ids.reshape(1, TOKENS),
        req_parent,
        mid_parent,
        node_len,
        residual,
        out_proj,
        norm_gain.reshape(1, -1),
        gate_proj.T,
        up_proj.T,
        down_proj,
        next_gain.reshape(1, -1),
        qkv_proj,
        qkv_bias,
    )


def solution(mesh):
    placed = (
        P("req", "mlp"),
        P("req", "mlp"),
        P("req", "mlp"),
        P("req", None, None, "mlp"),
        P(),
        P(),
        P("req"),
        P("req", None),
        P("req", None),
        P("req", None),
        P("req", None),
        P("mlp", None),
        P(),
        P(None, ("req", "mlp")),
        P(None, ("req", "mlp")),
        P(("req", "mlp"), None),
        P(),
        P(None, "mlp"),
        P("mlp"),
    )
    return jax.shard_map(
        body,
        mesh=mesh,
        in_specs=placed,
        out_specs=(P(("req", "mlp"), None), P("req", "mlp")),
        check_vma=False,
    )
```

```python
import functools
import math

import jax
import jax.numpy as jnp
from jax import lax
from jax.experimental import pallas as pl
from jax.experimental.pallas import tpu as pltpu
from jax.sharding import PartitionSpec as P

HEAD_SIZE = 128
QUERY_PER_KV = 5
REQ_DEV = 8
ROOT_DEV = 2
MID_DEV = 4
NODES_DEV = 6
NODE_MAX = 256
MODEL = 5120
ROWS = 16
UNITS = 108
UNITS_PAD = 128
DOWN_PAD = 112
QKV_COLS = 896
TOKENS = 128
PAGES = 32
PAGE = 64
ENTRIES = 24
PREFIX = NODES_DEV * NODE_MAX
SLICES = 5
CHUNKS = 4
HIDDEN = -1e30

EPS = 1e-06

MESH = pl.DeviceIdType.MESH


def place():
    req = lax.axis_index("req")
    mlp = lax.axis_index("mlp")
    return lax.div(mlp, 2), lax.div(req, 4), lax.rem(req, 4), lax.rem(mlp, 2)


def device(x, y, z, core):
    return (y * 4 + z, x * 2 + core)


def ahead(coords, axis, steps):
    moved = list(coords)
    moved[axis] = lax.rem(moved[axis] + steps, 4)
    return moved


def greet(others):
    barrier = pltpu.get_barrier_semaphore()
    for other in others:
        pl.semaphore_signal(barrier, inc=1, device_id=other, device_id_type=MESH)


def greeted(others):
    pl.semaphore_wait(pltpu.get_barrier_semaphore(), len(others))


def lines_through(x, y, z, core):
    others = [device(x, y, z, 1 - core)]
    for axis in range(3):
        for steps in (1, 2, 3):
            others.append(device(*ahead((x, y, z), axis, steps), core))
    return others


def remote(src, dst, send, recv, target):
    return pltpu.make_async_remote_copy(
        src_ref=src, dst_ref=dst, send_sem=send, recv_sem=recv, device_id=target, device_id_type=MESH
    )


def normed_rows(rows, gain):
    mean_sq = jnp.mean(rows * rows, axis=-1, keepdims=True)
    return (rows * lax.rsqrt(mean_sq + EPS) * gain).astype(jnp.bfloat16)


PARTS = (
    (0, 1024, 512, (1, 2, 0)),
    (1024, 2048, 1024, (0, 1, 2)),
    (3072, 2048, 1024, (0, 2, 1)),
)


def layer_kernel(
    queries,
    leaf_keys,
    leaf_values,
    pages_hbm,
    holder,
    slot,
    segment_row,
    req_parent,
    mid_parent,
    node_len,
    residual,
    out_hbm,
    gain,
    gate_hbm,
    up_hbm,
    down_hbm,
    next_gain,
    qkv_hbm,
    bias,
    layer_out,
    qkv_out,
    pages,
    outgoing,
    incoming,
    keys,
    values,
    hide,
    attention,
    out_proj,
    gate_up,
    own_down,
    projected,
    resid,
    half,
    summed,
    arrived,
    tokens,
    wide_weights,
    hidden,
    hidden_in,
    sums_f32,
    squares,
    down,
    local_sem,
    page_send,
    page_recv,
    half_send,
    half_recv,
    sum_send,
    sum_recv,
    weight_sem,
    part_send,
    part_recv,
    hid_send,
    hid_recv,
    down_send,
    down_recv,
    twin_send,
    twin_recv,
    first_send,
    first_recv,
    second_send,
    second_recv,
    row_send,
    row_recv,
):
    x, y, z, core = place()
    here = (x, y, z)
    group = lax.axis_index("req")
    sibling = device(x, y, z, 1 - core)
    own_rows = pl.multiple_of((x * 2 + core) * ROWS, ROWS)
    own_cols = pl.multiple_of(core * 2 * UNITS_PAD, 2 * UNITS_PAD)
    mine = x * 2 + core
    weights = wide_weights.at[:, 0 : 4 * UNITS_PAD]
    others = lines_through(x, y, z, core)
    plane = []
    for offset in range(1, 16):
        spot = (x, lax.rem(y + offset // 4, 4), lax.rem(z + offset % 4, 4))
        plane.append(spot)
        if offset // 4 and offset % 4:
            others.append(device(*spot, core))
    greet(others)

    def local(src, dst, index):
        copy = pltpu.make_async_copy(src, dst, local_sem.at[index])
        copy.start()
        return copy

    pages_copy = local(pages_hbm, pages, 0)
    down_copy = local(down_hbm, own_down, 5)
    gate_copy = local(gate_hbm, gate_up.at[0], 1)
    up_copy = local(up_hbm, gate_up.at[1], 2)
    out_copy = local(out_hbm, out_proj, 3)
    resid_copy = local(residual.at[pl.ds(own_rows, ROWS), :], resid, 4)

    pages_copy.wait()
    for number, spot in enumerate(plane):
        asker = spot[1] * 4 + spot[2]
        picked = jnp.int32(0)
        for entry in range(ENTRIES):
            picked = jnp.where(holder[entry // 4, entry % 4, asker] == group, slot[entry // 4, entry % 4, asker], picked)
        outgoing[number] = pages[picked]
    greeted(others)
    fetched = []
    for number in range(14, -1, -1):
        copy = remote(
            outgoing.at[number],
            incoming.at[group],
            page_send.at[number],
            page_recv.at[number],
            device(*plane[number], core),
        )
        copy.start()
        fetched.append(copy)

    twins = []
    downs = []

    def down_block(offset, first, width):
        member = lax.rem(x + offset, 4) * 2 + core
        return down.at[member, pl.ds(0, DOWN_PAD), pl.ds(first, width)]

    def down_push(kind, part, way, offset, first, width):
        view = down_block(offset, first, width)
        copy = remote(
            view,
            view,
            down_send.at[kind, part, way],
            down_recv.at[kind, part, way],
            device(*ahead(here, 0, (1, 3)[way]), core),
        )
        copy.start()
        downs.append(copy)
        return copy

    def twin(offset):
        view = down_block(offset, 0, MODEL)
        copy = remote(view, view, twin_send.at[offset], twin_recv.at[offset], sibling)
        copy.start()
        twins.append(copy)

    wide = MODEL // 2

    def down_direct(part):
        return [down_push(0, part, way, 0, part * wide, wide) for way in range(2)]

    def down_onward(part):
        return [
            down_push(1, part, way, behind, part * wide + way * (wide // 2), wide // 2)
            for way, behind in enumerate((3, 1))
        ]

    down_copy.wait()
    down[mine, pl.ds(0, DOWN_PAD), :] = jnp.concatenate(
        [own_down[...], jnp.zeros((DOWN_PAD - UNITS, MODEL), jnp.bfloat16)], axis=0
    )
    for member in range(8):
        down[member, pl.ds(DOWN_PAD, UNITS_PAD - DOWN_PAD), :] = jnp.zeros(
            (UNITS_PAD - DOWN_PAD, MODEL), jnp.bfloat16
        )
    down_near = [down_direct(0)]

    line = segment_row[...]
    across = lax.broadcasted_iota(jnp.int32, (TOKENS, TOKENS), 1)
    along = lax.broadcasted_iota(jnp.int32, (TOKENS, TOKENS), 0)
    segments = jnp.sum(jnp.where(across == along, line, 0), axis=1, keepdims=True)
    middle = jnp.zeros_like(segments)
    for request in range(REQ_DEV):
        middle = jnp.where(segments == request, req_parent[0, request], middle)
    root = jnp.zeros_like(segments)
    for node in range(MID_DEV):
        root = jnp.where(middle == node, mid_parent[0, node], root)
    position = lax.broadcasted_iota(jnp.int32, (TOKENS, NODE_MAX), 1)
    for node in range(NODES_DEV):
        chosen = root == node if node < ROOT_DEV else middle == node - ROOT_DEV
        length = jnp.where(chosen, node_len[0, node], 0)
        hide[:, node * NODE_MAX : (node + 1) * NODE_MAX] = jnp.where(position < length, 0.0, HIDDEN)
    hide[:, PREFIX:] = jnp.where((segments == line) & (across <= along), 0.0, HIDDEN)

    for copy in fetched:
        copy.wait_recv()
    for entry in range(ENTRIES):
        kept = holder[entry // 4, entry % 4, group]
        page = jnp.where(kept == group, pages[slot[entry // 4, entry % 4, group]], incoming[kept])
        keys[entry * PAGE : (entry + 1) * PAGE, :] = page[:, :HEAD_SIZE]
        values[entry * PAGE : (entry + 1) * PAGE, :] = page[:, HEAD_SIZE:]
    keys[PREFIX:, :] = leaf_keys[...]
    values[PREFIX:, :] = leaf_values[...]
    for head in range(QUERY_PER_KV):
        cols = slice(head * HEAD_SIZE, (head + 1) * HEAD_SIZE)
        score = lax.dot_general(
            queries[:, cols], keys[...], (((1,), (1,)), ((), ())), preferred_element_type=jnp.float32
        )
        score = score * (1.0 / math.sqrt(HEAD_SIZE)) + hide[...]
        expo = jnp.exp(score - jnp.max(score, axis=1, keepdims=True))
        total = jnp.sum(expo, axis=1, keepdims=True)
        seen = jnp.dot(expo.astype(jnp.bfloat16), values[...], preferred_element_type=jnp.float32)
        attention[:, cols] = (seen / total).astype(jnp.bfloat16)

    out_copy.wait()
    size = MODEL // SLICES
    halves = []
    for piece in range(SLICES):
        cols = slice(piece * size, (piece + 1) * size)
        term = jnp.dot(
            attention[...],
            out_proj[:, :, cols].reshape(QUERY_PER_KV * HEAD_SIZE, size),
            preferred_element_type=jnp.float32)
        term = term.astype(jnp.bfloat16).reshape(4, 2, ROWS, size)
        projected[0, :, :, cols] = term[:, 0]
        projected[1, :, :, cols] = term[:, 1]
        copy = remote(
            projected.at[1 - core, :, :, cols],
            half.at[:, :, cols],
            half_send.at[piece],
            half_recv.at[piece],
            sibling,
        )
        copy.start()
        halves.append(copy)
    sums = []
    for piece in range(SLICES):
        cols = slice(piece * size, (piece + 1) * size)
        halves[piece].wait_recv()
        passing = []
        for steps in (2, 1, 3):
            chip = lax.rem(x + steps, 4)
            summed[steps, :, cols] = (
                projected[core, chip, :, cols].astype(jnp.float32) + half[chip, :, cols].astype(jnp.float32)
            ).astype(jnp.bfloat16)
            copy = remote(
                summed.at[steps, :, cols],
                arrived.at[steps, :, cols],
                sum_send.at[piece, steps - 1],
                sum_recv.at[piece, steps - 1],
                device(*ahead(here, 0, steps), core),
            )
            copy.start()
            passing.append(copy)
        sums.append(passing)
    gate_copy.wait()
    up_copy.wait()
    for which in range(2):
        cols = pl.ds(pl.multiple_of(own_cols + which * UNITS_PAD, UNITS_PAD), UNITS_PAD)
        weights[:, cols] = jnp.concatenate(
            [
                (gate_up[which].astype(jnp.float32) * gain[...]).astype(jnp.bfloat16),
                jnp.zeros((UNITS_PAD - UNITS, MODEL), jnp.bfloat16),
            ],
            axis=0,
        ).T
    spot = weights.at[:, pl.ds(own_cols, 2 * UNITS_PAD)]
    swap = remote(spot, spot, weight_sem.at[0], weight_sem.at[1], sibling)
    swap.start()

    def block(part, offsets, half=None):
        first, width, cut, order = PARTS[part]
        if half is not None:
            first, width = ((first, cut), (first + cut, width - cut))[half]
        index = [slice(None)] * 3
        for axis, offset in zip(order, offsets):
            if offset is not None:
                index[axis] = lax.rem(here[axis] + offset, 4)
        return (index[0], index[1], index[2], slice(None), pl.ds(first, width))

    pending = []

    def push(part, phase, slot, way, spot):
        view = tokens.at[spot]
        copy = remote(
            view,
            view,
            part_send.at[part, phase, slot, way],
            part_recv.at[part, phase, slot, way],
            device(*ahead(here, PARTS[part][3][phase], (1, 3)[way]), core),
        )
        copy.start()
        pending.append(copy)
        return copy

    def both_ways(part, phase, slot, offsets):
        spot = block(part, offsets)
        return [push(part, phase, slot, way, spot) for way in range(2)]

    def onward(part, phase, slot, offsets):
        return [
            push(part, phase, slot, way, block(part, offsets[:phase] + (behind,) + offsets[phase + 1 :], way))
            for way, behind in enumerate((3, 1))
        ]

    def arrive(copies):
        for copy in copies:
            copy.wait_recv()

    def product(part, offset):
        first, width, _, order = PARTS[part]
        index = [slice(None)] * 3
        index[order[2]] = lax.rem(here[order[2]] + offset, 4)
        rows = tokens[index[0], index[1], index[2], :, pl.ds(first, width)].reshape(256, width)
        exact = rows.astype(jnp.float32)
        square = jnp.broadcast_to(jnp.sum(exact * exact, axis=1, keepdims=True), (256, HEAD_SIZE))
        term = jnp.dot(rows, wide_weights[pl.ds(first, width), 0 : 4 * UNITS_PAD], preferred_element_type=jnp.float32)
        spot = (index[0], index[1], index[2])
        shape = [4, 4, 4]
        del shape[order[2]]
        sums_f32[spot] += term.reshape(*shape, ROWS, 4 * UNITS_PAD)
        squares[spot] += square.reshape(*shape, ROWS, HEAD_SIZE)

    every = range(3)
    near, lines = [], []
    resid_copy.wait()
    for piece in range(SLICES):
        cols = slice(piece * size, (piece + 1) * size)
        arrive(sums[piece])
        total = projected[core, x, :, cols].astype(jnp.float32) + half[x, :, cols].astype(jnp.float32)
        for steps in (1, 2, 3):
            total = total + arrived[steps, :, cols].astype(jnp.float32)
        stream = (resid[:, cols].astype(jnp.float32) + total).astype(jnp.bfloat16)
        resid[:, cols] = stream
        tokens[x, y, z, :, cols] = stream
        if piece % 2 == 0:
            near.append(both_ways(piece // 2, 0, 0, (0, 0, 0)))
            lines.append(both_ways(piece // 2, 1, 0, (0, 0, 0)))
    sums_f32[...] = jnp.zeros_like(sums_f32)
    squares[...] = jnp.zeros_like(squares)
    far = []
    for part in every:
        arrive(near[part])
        far.append(onward(part, 0, 1, (0, 0, 0)))
        for slot, offset in ((1, 1), (2, 3)):
            lines[part] += both_ways(part, 1, slot, (offset, 0, 0))
    planes = [[None] * 4 for _ in every]
    for part in every:
        arrive(far[part])
        lines[part] += both_ways(part, 1, 3, (2, 0, 0))
        planes[part][0] = both_ways(part, 2, 0, (None, 0, 0))
    arrive(down_near[0])
    down_far = down_onward(0)
    down_near.append(down_direct(1))
    twin(0)
    far = []
    for part in every:
        arrive(lines[part])
        far.append(onward(part, 1, 4, (None, 0, 0)))
        for offset in (1, 3):
            planes[part][offset] = both_ways(part, 2, offset, (None, offset, 0))
    for part in every:
        arrive(far[part])
        planes[part][2] = both_ways(part, 2, 2, (None, 2, 0))
    swap.wait_recv()
    last = []
    for offset in (0, 1, 3, 2):
        for part in every:
            arrive(planes[part][offset])
            last += onward(part, 2, 4 + offset, (None, offset, 0))
        if offset in (0, 1, 3):
            product((0, 1, None, 2)[offset], 0)
        if offset == 1:
            arrive(down_near[1])
            down_far += down_onward(1)
            twin(1)
            twin(3)
    for part in every:
        product(part, 1)
        product(part, 3)
    arrive(down_far)
    twin(2)
    arrive(last)
    for part in every:
        product(part, 2)

    swap.wait_send()
    qkv_copy = local(qkv_hbm, wide_weights, 6)
    given = []
    spot = hidden_in.at[:, pl.ds(pl.multiple_of(x * 2 * UNITS_PAD, 2 * UNITS_PAD), 2 * UNITS_PAD)]
    for steps in (2, 1, 3, 0):
        target = ahead(here, 0, steps)
        chip = target[0]
        factor = lax.rsqrt(squares[chip].reshape(256, HEAD_SIZE)[:, :1] * (1.0 / MODEL) + EPS)
        both = sums_f32[chip].reshape(256, 4 * UNITS_PAD) * factor
        outs = []
        for which in range(2):
            gate = both[:, which * 2 * UNITS_PAD : which * 2 * UNITS_PAD + UNITS_PAD]
            upper = both[:, which * 2 * UNITS_PAD + UNITS_PAD : (which + 1) * 2 * UNITS_PAD]
            outs.append((gate / (1.0 + jnp.exp(-gate)) * upper).astype(jnp.bfloat16))
        if steps:
            hidden[steps - 1] = jnp.concatenate(outs, axis=1)
            copy = remote(
                hidden.at[steps - 1], spot, hid_send.at[steps - 1], hid_recv.at[steps - 1], device(*target, core)
            )
            copy.start()
            given.append(copy)
        else:
            spot[...] = jnp.concatenate(outs, axis=1)
    for copy in pending:
        copy.wait_send()
    partial = tokens.at[0]
    rows = out_proj.at[0:8]
    second = out_proj.at[8:12]
    arrive(given)
    arrive(twins)

    size = MODEL // CHUNKS
    sent = []
    firsts = []
    for chunk in range(CHUNKS):
        cols = pl.ds(chunk * size, size)
        total = jnp.dot(
            hidden_in[...],
            down[:, :, chunk * size : (chunk + 1) * size].reshape(8 * UNITS_PAD, size),
            preferred_element_type=jnp.float32,
        )
        partial[:, :, :, cols] = total.astype(jnp.bfloat16).reshape(4, 4, ROWS, size)
        axis = 1 + chunk % 2
        copies = []
        for steps in (2, 1, 3):
            target = ahead(here, axis, steps)
            src = partial.at[target[1], :, :, cols] if axis == 1 else partial.at[:, target[2], :, cols]
            copy = remote(
                src,
                out_proj.at[4 * steps + 8 : 4 * steps + 12, :, cols],
                first_send.at[chunk, steps - 1],
                first_recv.at[chunk, steps - 1],
                device(*target, core),
            )
            copy.start()
            copies.append(copy)
        firsts.append(copies)
        sent += copies
    seconds = []
    for chunk in range(CHUNKS):
        cols = pl.ds(chunk * size, size)
        axis = 1 + chunk % 2
        for copy in firsts[chunk]:
            copy.wait_recv()
        own = partial[y, :, :, cols] if axis == 1 else partial[:, z, :, cols]
        total = own.astype(jnp.float32)
        for steps in range(3):
            total = total + out_proj[4 * steps + 12 : 4 * steps + 16, :, cols].astype(jnp.float32)
        second[:, :, cols] = total.astype(jnp.bfloat16)
        copies = []
        for steps in (2, 1, 3):
            target = ahead(here, 3 - axis, steps)
            copy = remote(
                second.at[target[3 - axis], :, cols],
                out_proj.at[23 + steps, :, cols],
                second_send.at[chunk, steps - 1],
                second_recv.at[chunk, steps - 1],
                device(*target, core),
            )
            copy.start()
            copies.append(copy)
        seconds.append(copies)
        sent += copies
    parts = []
    for chunk in range(CHUNKS):
        axis = 1 + chunk % 2
        for copy in seconds[chunk]:
            copy.wait_recv()
        cols = pl.ds(chunk * size, size)
        total = second[here[3 - axis], :, cols].astype(jnp.float32)
        for steps in range(3):
            total = total + out_proj[24 + steps, :, cols].astype(jnp.float32)
        parts.append(total)
    mixed = jnp.concatenate(parts, axis=1)
    out = (resid[...].astype(jnp.float32) + mixed).astype(jnp.bfloat16)
    layer_out[...] = out
    rows[mine] = normed_rows(out.astype(jnp.float32), next_gain[...])
    ring = []
    passed = []

    def hand(slot, member, part, target):
        view = rows.at[member, :, pl.ds(part * wide, wide)]
        copy = remote(view, view, row_send.at[part, slot], row_recv.at[part, slot], target)
        copy.start()
        return copy

    for part in range(2):
        ring.append([(steps, hand(steps - 1, mine, part, device(*ahead(here, 0, steps), core))) for steps in (2, 1, 3)])
        passed.append([hand(3, mine, part, sibling)])
    for part in range(2):
        for steps, arrival in reversed(ring[part]):
            arrival.wait_recv()
            other = lax.rem(x + 4 - steps, 4) * 2 + core
            passed[part].append(hand(3 + steps, other, part, sibling))
    qkv_copy.wait()
    result = bias[...].reshape(1, QKV_COLS)
    for part in range(2):
        arrive(passed[part])
        result = result + jnp.dot(
            rows[:, :, part * wide : (part + 1) * wide].reshape(TOKENS, wide),
            wide_weights[part * wide : (part + 1) * wide, :],
            preferred_element_type=jnp.float32,
        )
    qkv_out[...] = result.astype(jnp.bfloat16)
    for copy in fetched + halves + sum(sums, []) + downs + twins + given + sent + [copy for pair in ring for _, copy in pair] + sum(passed, []):
        copy.wait_send()


def layer(*operands):
    vmem = pl.BlockSpec(memory_space=pltpu.VMEM)
    smem = pl.BlockSpec(memory_space=pltpu.SMEM)
    anywhere = pl.BlockSpec(memory_space=pl.ANY)
    dma = pltpu.SemaphoreType.DMA

    def held(*shape):
        return pltpu.VMEM(shape, jnp.bfloat16)

    size = MODEL // CHUNKS
    return pl.pallas_call(
        layer_kernel,
        out_shape=(
            jax.ShapeDtypeStruct((ROWS, MODEL), jnp.bfloat16),
            jax.ShapeDtypeStruct((TOKENS, QKV_COLS), jnp.bfloat16),
        ),
        in_specs=[vmem] * 3
        + [anywhere, smem, smem, vmem, smem, smem, smem, anywhere, anywhere, vmem]
        + [anywhere, anywhere, anywhere, vmem, anywhere, vmem],
        out_specs=(vmem, vmem),
        scratch_shapes=[
            held(PAGES, PAGE, 2 * HEAD_SIZE),
            held(15, PAGE, 2 * HEAD_SIZE),
            held(16, PAGE, 2 * HEAD_SIZE),
            held(PREFIX + TOKENS, HEAD_SIZE),
            held(PREFIX + TOKENS, HEAD_SIZE),
            pltpu.VMEM((TOKENS, PREFIX + TOKENS), jnp.float32),
            held(TOKENS, QUERY_PER_KV * HEAD_SIZE),
            held(QUERY_PER_KV * HEAD_SIZE // ROWS, ROWS, MODEL),
            held(2, UNITS, MODEL),
            held(UNITS, MODEL),
            held(2, 4, ROWS, MODEL),
            held(ROWS, MODEL),
            held(4, ROWS, MODEL),
            held(4, ROWS, MODEL),
            held(4, ROWS, MODEL),
            held(4, 4, 4, ROWS, MODEL),
            held(MODEL, QKV_COLS),
            held(3, 256, 2 * UNITS_PAD),
            held(256, 8 * UNITS_PAD),
            pltpu.VMEM((4, 4, 4, ROWS, 4 * UNITS_PAD), jnp.float32),
            pltpu.VMEM((4, 4, 4, ROWS, HEAD_SIZE), jnp.float32),
            held(8, UNITS_PAD, MODEL),
            dma((7,)),
            dma((15,)),
            dma((15,)),
            dma((SLICES,)),
            dma((SLICES,)),
            dma((SLICES, 3)),
            dma((SLICES, 3)),
            dma((2,)),
            dma((3, 3, 8, 2)),
            dma((3, 3, 8, 2)),
            dma((3,)),
            dma((3,)),
            dma((2, 2, 2)),
            dma((2, 2, 2)),
            dma((4,)),
            dma((4,)),
            dma((CHUNKS, 3)),
            dma((CHUNKS, 3)),
            dma((CHUNKS, 3)),
            dma((CHUNKS, 3)),
            dma((2, 7)),
            dma((2, 7)),
        ],
        compiler_params=pltpu.CompilerParams(
            collective_id=0, has_side_effects=True, vmem_limit_bytes=51 << 20
        ),
        cost_estimate=pl.CostEstimate(flops=2 * 1024 * 5120 * 512, bytes_accessed=200 << 20, transcendentals=0),
    )(*operands)


def body(
    queries,
    leaf_keys,
    leaf_token_values,
    key_value_pages,
    page_holder,
    page_slot,
    segment_ids,
    req_parent,
    mid_parent,
    node_len,
    residual,
    out_proj,
    norm_gain,
    gate_proj,
    up_proj,
    down_proj,
    next_gain,
    qkv_proj,
    qkv_bias,
):
    return layer(
        queries,
        leaf_keys,
        leaf_token_values,
        key_value_pages.reshape(PAGES, PAGE, 2 * HEAD_SIZE),
        page_holder.transpose(1, 2, 0),
        page_slot.transpose(1, 2, 0),
        segment_ids.reshape(1, TOKENS),
        req_parent,
        mid_parent,
        node_len,
        residual,
        out_proj.reshape(QUERY_PER_KV * HEAD_SIZE // ROWS, ROWS, MODEL),
        norm_gain.reshape(1, -1),
        gate_proj.T,
        up_proj.T,
        down_proj,
        next_gain.reshape(1, -1),
        qkv_proj,
        qkv_bias,
    )


def solution(mesh):
    placed = (
        P("req", "mlp"),
        P("req", "mlp"),
        P("req", "mlp"),
        P("req", None, None, "mlp"),
        P(),
        P(),
        P("req"),
        P("req", None),
        P("req", None),
        P("req", None),
        P("req", None),
        P("mlp", None),
        P(),
        P(None, ("req", "mlp")),
        P(None, ("req", "mlp")),
        P(("req", "mlp"), None),
        P(),
        P(None, "mlp"),
        P("mlp"),
    )
    return jax.shard_map(
        body,
        mesh=mesh,
        in_specs=placed,
        out_specs=(P(("req", "mlp"), None), P("req", "mlp")),
        check_vma=False,
    )
```

```python
import functools
import math

import jax
import jax.numpy as jnp
from jax import lax
from jax.experimental import pallas as pl
from jax.experimental.pallas import tpu as pltpu
from jax.sharding import PartitionSpec as P

HEAD_SIZE = 128
QUERY_PER_KV = 5
REQ_DEV = 8
ROOT_DEV = 2
MID_DEV = 4
NODES_DEV = 6
NODE_MAX = 256
MODEL = 5120
ROWS = 16
UNITS = 108
UNITS_PAD = 128
DOWN_PAD = 112
QKV_COLS = 896
TOKENS = 128
PAGES = 32
PAGE = 64
ENTRIES = 24
PREFIX = NODES_DEV * NODE_MAX
SLICES = 5
CHUNKS = 8
HIDDEN = -1e30

EPS = 1e-06

MESH = pl.DeviceIdType.MESH


def place():
    req = lax.axis_index("req")
    mlp = lax.axis_index("mlp")
    return lax.div(mlp, 2), lax.div(req, 4), lax.rem(req, 4), lax.rem(mlp, 2)


def device(x, y, z, core):
    return (y * 4 + z, x * 2 + core)


def ahead(coords, axis, steps):
    moved = list(coords)
    moved[axis] = lax.rem(moved[axis] + steps, 4)
    return moved


def greet(others):
    barrier = pltpu.get_barrier_semaphore()
    for other in others:
        pl.semaphore_signal(barrier, inc=1, device_id=other, device_id_type=MESH)


def greeted(others):
    pl.semaphore_wait(pltpu.get_barrier_semaphore(), len(others))


def lines_through(x, y, z, core):
    others = [device(x, y, z, 1 - core)]
    for axis in range(3):
        for steps in (1, 2, 3):
            others.append(device(*ahead((x, y, z), axis, steps), core))
    return others


def remote(src, dst, send, recv, target):
    return pltpu.make_async_remote_copy(
        src_ref=src, dst_ref=dst, send_sem=send, recv_sem=recv, device_id=target, device_id_type=MESH
    )


def normed_rows(rows, gain):
    mean_sq = jnp.mean(rows * rows, axis=-1, keepdims=True)
    return (rows * lax.rsqrt(mean_sq + EPS) * gain).astype(jnp.bfloat16)


PARTS = (
    (0, 1024, 512, (1, 2, 0)),
    (1024, 2048, 1024, (0, 1, 2)),
    (3072, 2048, 1024, (0, 2, 1)),
)


def layer_kernel(
    queries,
    leaf_keys,
    leaf_values,
    pages_hbm,
    holder,
    slot,
    segment_row,
    req_parent,
    mid_parent,
    node_len,
    residual,
    out_hbm,
    gain,
    gate_hbm,
    up_hbm,
    down_hbm,
    next_gain,
    qkv_hbm,
    bias,
    layer_out,
    qkv_out,
    pages,
    outgoing,
    incoming,
    keys,
    values,
    hide,
    attention,
    out_proj,
    gate_up,
    own_down,
    projected,
    resid,
    half,
    summed,
    arrived,
    tokens,
    wide_weights,
    hidden,
    hidden_in,
    sums_f32,
    squares,
    down,
    local_sem,
    page_send,
    page_recv,
    half_send,
    half_recv,
    sum_send,
    sum_recv,
    weight_sem,
    part_send,
    part_recv,
    hid_send,
    hid_recv,
    down_send,
    down_recv,
    twin_send,
    twin_recv,
    first_send,
    first_recv,
    second_send,
    second_recv,
    row_send,
    row_recv,
):
    x, y, z, core = place()
    here = (x, y, z)
    group = lax.axis_index("req")
    sibling = device(x, y, z, 1 - core)
    own_rows = pl.multiple_of((x * 2 + core) * ROWS, ROWS)
    own_cols = pl.multiple_of(core * 2 * UNITS_PAD, 2 * UNITS_PAD)
    mine = x * 2 + core
    weights = wide_weights.at[:, 0 : 4 * UNITS_PAD]
    others = lines_through(x, y, z, core)
    plane = []
    for offset in range(1, 16):
        spot = (x, lax.rem(y + offset // 4, 4), lax.rem(z + offset % 4, 4))
        plane.append(spot)
        if offset // 4 and offset % 4:
            others.append(device(*spot, core))
    greet(others)

    def local(src, dst, index):
        copy = pltpu.make_async_copy(src, dst, local_sem.at[index])
        copy.start()
        return copy

    pages_copy = local(pages_hbm, pages, 0)
    down_copy = local(down_hbm, own_down, 5)
    gate_copy = local(gate_hbm, gate_up.at[0], 1)
    up_copy = local(up_hbm, gate_up.at[1], 2)
    out_copy = local(out_hbm, out_proj, 3)
    resid_copy = local(residual.at[pl.ds(own_rows, ROWS), :], resid, 4)

    pages_copy.wait()
    for number, spot in enumerate(plane):
        asker = spot[1] * 4 + spot[2]
        picked = jnp.int32(0)
        for entry in range(ENTRIES):
            picked = jnp.where(holder[entry // 4, entry % 4, asker] == group, slot[entry // 4, entry % 4, asker], picked)
        outgoing[number] = pages[picked]
    greeted(others)
    fetched = []
    for number in range(14, -1, -1):
        copy = remote(
            outgoing.at[number],
            incoming.at[group],
            page_send.at[number],
            page_recv.at[number],
            device(*plane[number], core),
        )
        copy.start()
        fetched.append(copy)

    twins = []
    downs = []

    def down_block(offset, first, width):
        member = lax.rem(x + offset, 4) * 2 + core
        return down.at[member, pl.ds(0, DOWN_PAD), pl.ds(first, width)]

    def down_push(kind, part, way, offset, first, width):
        view = down_block(offset, first, width)
        copy = remote(
            view,
            view,
            down_send.at[kind, part, way],
            down_recv.at[kind, part, way],
            device(*ahead(here, 0, (1, 3)[way]), core),
        )
        copy.start()
        downs.append(copy)
        return copy

    def twin(offset):
        view = down_block(offset, 0, MODEL)
        copy = remote(view, view, twin_send.at[offset], twin_recv.at[offset], sibling)
        copy.start()
        twins.append(copy)

    wide = MODEL // 2

    def down_direct(part):
        return [down_push(0, part, way, 0, part * wide, wide) for way in range(2)]

    def down_onward(part):
        return [
            down_push(1, part, way, behind, part * wide + way * (wide // 2), wide // 2)
            for way, behind in enumerate((3, 1))
        ]

    down_copy.wait()
    down[mine, pl.ds(0, DOWN_PAD), :] = jnp.concatenate(
        [own_down[...], jnp.zeros((DOWN_PAD - UNITS, MODEL), jnp.bfloat16)], axis=0
    )
    for member in range(8):
        down[member, pl.ds(DOWN_PAD, UNITS_PAD - DOWN_PAD), :] = jnp.zeros(
            (UNITS_PAD - DOWN_PAD, MODEL), jnp.bfloat16
        )
    down_near = [down_direct(0)]

    line = segment_row[...]
    across = lax.broadcasted_iota(jnp.int32, (TOKENS, TOKENS), 1)
    along = lax.broadcasted_iota(jnp.int32, (TOKENS, TOKENS), 0)
    segments = jnp.sum(jnp.where(across == along, line, 0), axis=1, keepdims=True)
    middle = jnp.zeros_like(segments)
    for request in range(REQ_DEV):
        middle = jnp.where(segments == request, req_parent[0, request], middle)
    root = jnp.zeros_like(segments)
    for node in range(MID_DEV):
        root = jnp.where(middle == node, mid_parent[0, node], root)
    position = lax.broadcasted_iota(jnp.int32, (TOKENS, NODE_MAX), 1)
    for node in range(NODES_DEV):
        chosen = root == node if node < ROOT_DEV else middle == node - ROOT_DEV
        length = jnp.where(chosen, node_len[0, node], 0)
        hide[:, node * NODE_MAX : (node + 1) * NODE_MAX] = jnp.where(position < length, 0.0, HIDDEN)
    hide[:, PREFIX:] = jnp.where((segments == line) & (across <= along), 0.0, HIDDEN)

    for copy in fetched:
        copy.wait_recv()
    for entry in range(ENTRIES):
        kept = holder[entry // 4, entry % 4, group]
        page = jnp.where(kept == group, pages[slot[entry // 4, entry % 4, group]], incoming[kept])
        keys[entry * PAGE : (entry + 1) * PAGE, :] = page[:, :HEAD_SIZE]
        values[entry * PAGE : (entry + 1) * PAGE, :] = page[:, HEAD_SIZE:]
    keys[PREFIX:, :] = leaf_keys[...]
    values[PREFIX:, :] = leaf_values[...]
    for head in range(QUERY_PER_KV):
        cols = slice(head * HEAD_SIZE, (head + 1) * HEAD_SIZE)
        score = lax.dot_general(
            queries[:, cols], keys[...], (((1,), (1,)), ((), ())), preferred_element_type=jnp.float32
        )
        score = score * (1.0 / math.sqrt(HEAD_SIZE)) + hide[...]
        expo = jnp.exp(score - jnp.max(score, axis=1, keepdims=True))
        total = jnp.sum(expo, axis=1, keepdims=True)
        seen = jnp.dot(expo.astype(jnp.bfloat16), values[...], preferred_element_type=jnp.float32)
        attention[:, cols] = (seen / total).astype(jnp.bfloat16)

    out_copy.wait()
    size = MODEL // SLICES
    halves = []
    for piece in range(SLICES):
        cols = slice(piece * size, (piece + 1) * size)
        term = jnp.dot(
            attention[...],
            out_proj[:, :, cols].reshape(QUERY_PER_KV * HEAD_SIZE, size),
            preferred_element_type=jnp.float32)
        term = term.astype(jnp.bfloat16).reshape(4, 2, ROWS, size)
        projected[0, :, :, cols] = term[:, 0]
        projected[1, :, :, cols] = term[:, 1]
        copy = remote(
            projected.at[1 - core, :, :, cols],
            half.at[:, :, cols],
            half_send.at[piece],
            half_recv.at[piece],
            sibling,
        )
        copy.start()
        halves.append(copy)
    sums = []
    for piece in range(SLICES):
        cols = slice(piece * size, (piece + 1) * size)
        halves[piece].wait_recv()
        passing = []
        for steps in (2, 1, 3):
            chip = lax.rem(x + steps, 4)
            summed[steps, :, cols] = (
                projected[core, chip, :, cols].astype(jnp.float32) + half[chip, :, cols].astype(jnp.float32)
            ).astype(jnp.bfloat16)
            copy = remote(
                summed.at[steps, :, cols],
                arrived.at[steps, :, cols],
                sum_send.at[piece, steps - 1],
                sum_recv.at[piece, steps - 1],
                device(*ahead(here, 0, steps), core),
            )
            copy.start()
            passing.append(copy)
        sums.append(passing)
    gate_copy.wait()
    up_copy.wait()
    for which in range(2):
        cols = pl.ds(pl.multiple_of(own_cols + which * UNITS_PAD, UNITS_PAD), UNITS_PAD)
        weights[:, cols] = jnp.concatenate(
            [
                (gate_up[which].astype(jnp.float32) * gain[...]).astype(jnp.bfloat16),
                jnp.zeros((UNITS_PAD - UNITS, MODEL), jnp.bfloat16),
            ],
            axis=0,
        ).T
    spot = weights.at[:, pl.ds(own_cols, 2 * UNITS_PAD)]
    swap = remote(spot, spot, weight_sem.at[0], weight_sem.at[1], sibling)
    swap.start()

    def block(part, offsets, half=None):
        first, width, cut, order = PARTS[part]
        if half is not None:
            first, width = ((first, cut), (first + cut, width - cut))[half]
        index = [slice(None)] * 3
        for axis, offset in zip(order, offsets):
            if offset is not None:
                index[axis] = lax.rem(here[axis] + offset, 4)
        return (index[0], index[1], index[2], slice(None), pl.ds(first, width))

    pending = []

    def push(part, phase, slot, way, spot):
        view = tokens.at[spot]
        copy = remote(
            view,
            view,
            part_send.at[part, phase, slot, way],
            part_recv.at[part, phase, slot, way],
            device(*ahead(here, PARTS[part][3][phase], (1, 3)[way]), core),
        )
        copy.start()
        pending.append(copy)
        return copy

    def both_ways(part, phase, slot, offsets):
        spot = block(part, offsets)
        return [push(part, phase, slot, way, spot) for way in range(2)]

    def onward(part, phase, slot, offsets):
        return [
            push(part, phase, slot, way, block(part, offsets[:phase] + (behind,) + offsets[phase + 1 :], way))
            for way, behind in enumerate((3, 1))
        ]

    def arrive(copies):
        for copy in copies:
            copy.wait_recv()

    def product(part, offset):
        first, width, _, order = PARTS[part]
        index = [slice(None)] * 3
        index[order[2]] = lax.rem(here[order[2]] + offset, 4)
        rows = tokens[index[0], index[1], index[2], :, pl.ds(first, width)].reshape(256, width)
        exact = rows.astype(jnp.float32)
        square = jnp.broadcast_to(jnp.sum(exact * exact, axis=1, keepdims=True), (256, HEAD_SIZE))
        term = jnp.dot(rows, wide_weights[pl.ds(first, width), 0 : 4 * UNITS_PAD], preferred_element_type=jnp.float32)
        spot = (index[0], index[1], index[2])
        shape = [4, 4, 4]
        del shape[order[2]]
        sums_f32[spot] += term.reshape(*shape, ROWS, 4 * UNITS_PAD)
        squares[spot] += square.reshape(*shape, ROWS, HEAD_SIZE)

    every = range(3)
    near, lines = [], []
    resid_copy.wait()
    for piece in range(SLICES):
        cols = slice(piece * size, (piece + 1) * size)
        arrive(sums[piece])
        total = projected[core, x, :, cols].astype(jnp.float32) + half[x, :, cols].astype(jnp.float32)
        for steps in (1, 2, 3):
            total = total + arrived[steps, :, cols].astype(jnp.float32)
        stream = (resid[:, cols].astype(jnp.float32) + total).astype(jnp.bfloat16)
        resid[:, cols] = stream
        tokens[x, y, z, :, cols] = stream
        if piece % 2 == 0:
            near.append(both_ways(piece // 2, 0, 0, (0, 0, 0)))
            lines.append(both_ways(piece // 2, 1, 0, (0, 0, 0)))
    sums_f32[...] = jnp.zeros_like(sums_f32)
    squares[...] = jnp.zeros_like(squares)
    far = []
    for part in every:
        arrive(near[part])
        far.append(onward(part, 0, 1, (0, 0, 0)))
        for slot, offset in ((1, 1), (2, 3)):
            lines[part] += both_ways(part, 1, slot, (offset, 0, 0))
    planes = [[None] * 4 for _ in every]
    for part in every:
        arrive(far[part])
        lines[part] += both_ways(part, 1, 3, (2, 0, 0))
        planes[part][0] = both_ways(part, 2, 0, (None, 0, 0))
    arrive(down_near[0])
    down_far = down_onward(0)
    down_near.append(down_direct(1))
    twin(0)
    far = []
    for part in every:
        arrive(lines[part])
        far.append(onward(part, 1, 4, (None, 0, 0)))
        for offset in (1, 3):
            planes[part][offset] = both_ways(part, 2, offset, (None, offset, 0))
    for part in every:
        arrive(far[part])
        planes[part][2] = both_ways(part, 2, 2, (None, 2, 0))
    swap.wait_recv()
    last = []
    for offset in (0, 1, 3, 2):
        for part in every:
            arrive(planes[part][offset])
            last += onward(part, 2, 4 + offset, (None, offset, 0))
        if offset in (0, 1, 3):
            product((0, 1, None, 2)[offset], 0)
        if offset == 1:
            arrive(down_near[1])
            down_far += down_onward(1)
            twin(1)
            twin(3)
    for part in every:
        product(part, 1)
        product(part, 3)
    arrive(down_far)
    twin(2)
    arrive(last)
    for part in every:
        product(part, 2)

    swap.wait_send()
    qkv_copy = local(qkv_hbm, wide_weights, 6)
    given = []
    spot = hidden_in.at[:, pl.ds(pl.multiple_of(x * 2 * UNITS_PAD, 2 * UNITS_PAD), 2 * UNITS_PAD)]
    for steps in (2, 1, 3, 0):
        target = ahead(here, 0, steps)
        chip = target[0]
        factor = lax.rsqrt(squares[chip].reshape(256, HEAD_SIZE)[:, :1] * (1.0 / MODEL) + EPS)
        both = sums_f32[chip].reshape(256, 4 * UNITS_PAD) * factor
        outs = []
        for which in range(2):
            gate = both[:, which * 2 * UNITS_PAD : which * 2 * UNITS_PAD + UNITS_PAD]
            upper = both[:, which * 2 * UNITS_PAD + UNITS_PAD : (which + 1) * 2 * UNITS_PAD]
            outs.append((gate / (1.0 + jnp.exp(-gate)) * upper).astype(jnp.bfloat16))
        if steps:
            hidden[steps - 1] = jnp.concatenate(outs, axis=1)
            copy = remote(
                hidden.at[steps - 1], spot, hid_send.at[steps - 1], hid_recv.at[steps - 1], device(*target, core)
            )
            copy.start()
            given.append(copy)
        else:
            spot[...] = jnp.concatenate(outs, axis=1)
    for copy in pending:
        copy.wait_send()
    partial = tokens.at[0]
    rows = out_proj.at[0:8]
    second = out_proj.at[8:12]
    arrive(given)
    arrive(twins)

    size = MODEL // CHUNKS
    sent = []
    firsts = []
    for chunk in range(CHUNKS):
        cols = pl.ds(chunk * size, size)
        total = jnp.dot(
            hidden_in[...],
            down[:, :, chunk * size : (chunk + 1) * size].reshape(8 * UNITS_PAD, size),
            preferred_element_type=jnp.float32,
        )
        partial[:, :, :, cols] = total.astype(jnp.bfloat16).reshape(4, 4, ROWS, size)
        axis = 1 + chunk % 2
        copies = []
        for steps in (2, 1, 3):
            target = ahead(here, axis, steps)
            src = partial.at[target[1], :, :, cols] if axis == 1 else partial.at[:, target[2], :, cols]
            copy = remote(
                src,
                out_proj.at[4 * steps + 8 : 4 * steps + 12, :, cols],
                first_send.at[chunk, steps - 1],
                first_recv.at[chunk, steps - 1],
                device(*target, core),
            )
            copy.start()
            copies.append(copy)
        firsts.append(copies)
        sent += copies
    seconds = []
    for chunk in range(CHUNKS):
        cols = pl.ds(chunk * size, size)
        axis = 1 + chunk % 2
        for copy in firsts[chunk]:
            copy.wait_recv()
        own = partial[y, :, :, cols] if axis == 1 else partial[:, z, :, cols]
        total = own.astype(jnp.float32)
        for steps in range(3):
            total = total + out_proj[4 * steps + 12 : 4 * steps + 16, :, cols].astype(jnp.float32)
        second[:, :, cols] = total.astype(jnp.bfloat16)
        copies = []
        for steps in (2, 1, 3):
            target = ahead(here, 3 - axis, steps)
            copy = remote(
                second.at[target[3 - axis], :, cols],
                out_proj.at[23 + steps, :, cols],
                second_send.at[chunk, steps - 1],
                second_recv.at[chunk, steps - 1],
                device(*target, core),
            )
            copy.start()
            copies.append(copy)
        seconds.append(copies)
        sent += copies
    parts = []
    for chunk in range(CHUNKS):
        axis = 1 + chunk % 2
        for copy in seconds[chunk]:
            copy.wait_recv()
        cols = pl.ds(chunk * size, size)
        total = second[here[3 - axis], :, cols].astype(jnp.float32)
        for steps in range(3):
            total = total + out_proj[24 + steps, :, cols].astype(jnp.float32)
        parts.append(total)
    mixed = jnp.concatenate(parts, axis=1)
    out = (resid[...].astype(jnp.float32) + mixed).astype(jnp.bfloat16)
    layer_out[...] = out
    rows[mine] = normed_rows(out.astype(jnp.float32), next_gain[...])
    ring = []
    passed = []

    def hand(slot, member, part, target):
        view = rows.at[member, :, pl.ds(part * wide, wide)]
        copy = remote(view, view, row_send.at[part, slot], row_recv.at[part, slot], target)
        copy.start()
        return copy

    for part in range(2):
        ring.append([(steps, hand(steps - 1, mine, part, device(*ahead(here, 0, steps), core))) for steps in (2, 1, 3)])
        passed.append([hand(3, mine, part, sibling)])
    for part in range(2):
        for steps, arrival in reversed(ring[part]):
            arrival.wait_recv()
            other = lax.rem(x + 4 - steps, 4) * 2 + core
            passed[part].append(hand(3 + steps, other, part, sibling))
    qkv_copy.wait()
    result = bias[...].reshape(1, QKV_COLS)
    for part in range(2):
        arrive(passed[part])
        result = result + jnp.dot(
            rows[:, :, part * wide : (part + 1) * wide].reshape(TOKENS, wide),
            wide_weights[part * wide : (part + 1) * wide, :],
            preferred_element_type=jnp.float32,
        )
    qkv_out[...] = result.astype(jnp.bfloat16)
    for copy in fetched + halves + sum(sums, []) + downs + twins + given + sent + [copy for pair in ring for _, copy in pair] + sum(passed, []):
        copy.wait_send()


def layer(*operands):
    vmem = pl.BlockSpec(memory_space=pltpu.VMEM)
    smem = pl.BlockSpec(memory_space=pltpu.SMEM)
    anywhere = pl.BlockSpec(memory_space=pl.ANY)
    dma = pltpu.SemaphoreType.DMA

    def held(*shape):
        return pltpu.VMEM(shape, jnp.bfloat16)

    size = MODEL // CHUNKS
    return pl.pallas_call(
        layer_kernel,
        out_shape=(
            jax.ShapeDtypeStruct((ROWS, MODEL), jnp.bfloat16),
            jax.ShapeDtypeStruct((TOKENS, QKV_COLS), jnp.bfloat16),
        ),
        in_specs=[vmem] * 3
        + [anywhere, smem, smem, vmem, smem, smem, smem, anywhere, anywhere, vmem]
        + [anywhere, anywhere, anywhere, vmem, anywhere, vmem],
        out_specs=(vmem, vmem),
        scratch_shapes=[
            held(PAGES, PAGE, 2 * HEAD_SIZE),
            held(15, PAGE, 2 * HEAD_SIZE),
            held(16, PAGE, 2 * HEAD_SIZE),
            held(PREFIX + TOKENS, HEAD_SIZE),
            held(PREFIX + TOKENS, HEAD_SIZE),
            pltpu.VMEM((TOKENS, PREFIX + TOKENS), jnp.float32),
            held(TOKENS, QUERY_PER_KV * HEAD_SIZE),
            held(QUERY_PER_KV * HEAD_SIZE // ROWS, ROWS, MODEL),
            held(2, UNITS, MODEL),
            held(UNITS, MODEL),
            held(2, 4, ROWS, MODEL),
            held(ROWS, MODEL),
            held(4, ROWS, MODEL),
            held(4, ROWS, MODEL),
            held(4, ROWS, MODEL),
            held(4, 4, 4, ROWS, MODEL),
            held(MODEL, QKV_COLS),
            held(3, 256, 2 * UNITS_PAD),
            held(256, 8 * UNITS_PAD),
            pltpu.VMEM((4, 4, 4, ROWS, 4 * UNITS_PAD), jnp.float32),
            pltpu.VMEM((4, 4, 4, ROWS, HEAD_SIZE), jnp.float32),
            held(8, UNITS_PAD, MODEL),
            dma((7,)),
            dma((15,)),
            dma((15,)),
            dma((SLICES,)),
            dma((SLICES,)),
            dma((SLICES, 3)),
            dma((SLICES, 3)),
            dma((2,)),
            dma((3, 3, 8, 2)),
            dma((3, 3, 8, 2)),
            dma((3,)),
            dma((3,)),
            dma((2, 2, 2)),
            dma((2, 2, 2)),
            dma((4,)),
            dma((4,)),
            dma((CHUNKS, 3)),
            dma((CHUNKS, 3)),
            dma((CHUNKS, 3)),
            dma((CHUNKS, 3)),
            dma((2, 7)),
            dma((2, 7)),
        ],
        compiler_params=pltpu.CompilerParams(
            collective_id=0, has_side_effects=True, vmem_limit_bytes=51 << 20
        ),
        cost_estimate=pl.CostEstimate(flops=2 * 1024 * 5120 * 512, bytes_accessed=200 << 20, transcendentals=0),
    )(*operands)


def body(
    queries,
    leaf_keys,
    leaf_token_values,
    key_value_pages,
    page_holder,
    page_slot,
    segment_ids,
    req_parent,
    mid_parent,
    node_len,
    residual,
    out_proj,
    norm_gain,
    gate_proj,
    up_proj,
    down_proj,
    next_gain,
    qkv_proj,
    qkv_bias,
):
    return layer(
        queries,
        leaf_keys,
        leaf_token_values,
        key_value_pages.reshape(PAGES, PAGE, 2 * HEAD_SIZE),
        page_holder.transpose(1, 2, 0),
        page_slot.transpose(1, 2, 0),
        segment_ids.reshape(1, TOKENS),
        req_parent,
        mid_parent,
        node_len,
        residual,
        out_proj.reshape(QUERY_PER_KV * HEAD_SIZE // ROWS, ROWS, MODEL),
        norm_gain.reshape(1, -1),
        gate_proj.T,
        up_proj.T,
        down_proj,
        next_gain.reshape(1, -1),
        qkv_proj,
        qkv_bias,
    )


def solution(mesh):
    placed = (
        P("req", "mlp"),
        P("req", "mlp"),
        P("req", "mlp"),
        P("req", None, None, "mlp"),
        P(),
        P(),
        P("req"),
        P("req", None),
        P("req", None),
        P("req", None),
        P("req", None),
        P("mlp", None),
        P(),
        P(None, ("req", "mlp")),
        P(None, ("req", "mlp")),
        P(("req", "mlp"), None),
        P(),
        P(None, "mlp"),
        P("mlp"),
    )
    return jax.shard_map(
        body,
        mesh=mesh,
        in_specs=placed,
        out_specs=(P(("req", "mlp"), None), P("req", "mlp")),
        check_vma=False,
    )
```
